32 devices in a mesh: ctx: 8 (over z, x), fsdp: 2 (over y), dp: 2 (over core).
Axes of the slice: x: 2, y: 2, z: 4, core: 2. Of those that a mesh axis runs over, the one named last changes fastest.
Arguments:
- inputs: bfloat16 [4, 1024, 4096], P(('fsdp', 'dp'), 'ctx'), may hold values from -6 to 6
- queries: bfloat16 [4, 1024, 4096], P(('fsdp', 'dp'), 'ctx'), may hold values from -40 to 40, as said below
- w_kv: bfloat16 [4096, 1024], P(('ctx', 'fsdp')), may hold values from -0.09375 to 0.09375
- tile_mask: int32 [8, 4], P('ctx'), may hold values from 0 to 1, as said below
- grad_out: bfloat16 [4, 1024, 4096], P(('fsdp', 'dp'), 'ctx'), may hold values from -6 to 6
Outputs:
- attn_out: bfloat16 [4, 1024, 4096], P(('fsdp', 'dp'), 'ctx')
- grad_queries: bfloat16 [4, 1024, 4096], P(('fsdp', 'dp'), 'ctx')
- grad_inputs: bfloat16 [4, 1024, 4096], P(('fsdp', 'dp'), 'ctx')
- grad_weights: float32 [4096, 1024], P(('ctx', 'fsdp'))
The draws below stay inside these ranges and needn't reach their ends.
Inputs may be any that keep to these rules, and one draw needn't show every extreme that they name: tile_mask[b, j] = 1 marks that query tile b scores key tile b - j - 1 in full; it is 0 where b - j - 1 < 0. The tiles of at least one token shard, drawn from the seed, score all earlier tiles within reach, the others few of them. `queries`: entries of order one, on some draws some rows larger.
All inputs are finite; a program needn't handle non-finite values.
Results may differ from the reference program's by a relative error of at most 0.015.
The reference program's roundings to bfloat16 on the way (of `key_vals`, `prob_bf16`, `grad_score` and `grad_kv`) count: a program that leaves them out, or rounds other values in their place, can miss the bound.
Values may be sent and summed in bfloat16 or wider, within the bound.
No kernel may reach another device: no remote copies, remote signals or barrier semaphores. Data moves between devices by JAX's collectives and lax.ppermute only.
A program may use at most 128 MiB of HBM per device.

```python
import math
import jax
import jax.numpy as jnp
from jax import lax

D = 4096
HEADS = 32
KV_HEADS = 4
HEAD_DIM = 128
BLOCK = 128
REACH = 4
TOK = 128
QW = 4096
KW = 512
SEQS = 4
SEQ_LEN = 1024
NBLK = 8
REACH_BLK = 4


def draw_queries(key, part):
    key_base = jax.random.fold_in(key, 11)
    base_draw = jnp.clip(jax.random.normal(key_base, (SEQS, SEQ_LEN, QW), jnp.float32), -4.0, 4.0)
    return base_draw.astype(jnp.bfloat16)


def draw_tile_mask(key, part):
    key_order = jax.random.fold_in(key, 21)
    key_coin = jax.random.fold_in(key, 22)
    per_shard = TOK // BLOCK
    shard_count = NBLK // per_shard
    shard_order = jax.random.permutation(key_order, shard_count)
    heavy_shard = shard_order < max(1, shard_count // 8)
    heavy_block = jnp.broadcast_to(heavy_shard[:, None], (shard_count, per_shard)).reshape(NBLK)
    coin_flip = jax.random.randint(key_coin, (NBLK, REACH_BLK), 0, 6) == 0
    block_index = jnp.arange(NBLK, dtype=jnp.int32)[:, None]
    back_steps = jnp.arange(1, REACH_BLK + 1, dtype=jnp.int32)[None, :]
    tile_flag = (heavy_block[:, None] | coin_flip) & (block_index - back_steps >= 0)
    return tile_flag.astype(jnp.int32)


def with_spikes(drawn, key, source, target, shards_of, factor):
    def block_of(dim):
        return (jnp.arange(drawn.shape[dim]) // (drawn.shape[dim] // shards_of)).reshape((-1,) + (1,) * (drawn.ndim - 1 - dim))

    near = jax.random.permutation(key, shards_of)[block_of(target)]
    other_side = (block_of(target) + shards_of // 2) % shards_of
    return jnp.where((block_of(source) == near) | (block_of(source) == other_side), factor * drawn, drawn)


def block_levels(rng, dims, pieces, smallest, high):
    level = 1.0
    for axis_at, shards_of in pieces:
        steps = jax.random.uniform(jax.random.fold_in(jax.random.fold_in(rng, 6), axis_at), (shards_of,), jnp.float32, smallest / len(pieces), high / len(pieces))
        level = level * jnp.repeat(jnp.exp(steps), dims[axis_at] // shards_of).reshape((-1,) + (1,) * (len(dims) - 1 - axis_at))
    return level


def scatter_about(rng, shape, deviation, limit, cuts=(), kind=jnp.bfloat16):
    gain = block_levels(rng, shape, cuts, -0.22, 0.18) if cuts else 1.0
    array = jax.random.normal(rng, shape, jnp.float32) * deviation * gain
    return jnp.minimum(jnp.maximum(array, -limit), limit).astype(kind)


def noise_with(rng, extent, spread, most, cuts, heavy, held_as=jnp.bfloat16):
    array = spread * jax.random.normal(rng, extent, jnp.float32)
    if cuts:
        array = array * block_levels(rng, extent, cuts, -0.22, 0.18)
    return jnp.clip(with_spikes(array, jax.random.fold_in(rng, 3), *heavy), -most, most).astype(held_as)


def setup_inputs(seed: int = 0) -> dict:
    seeds = jax.random.split(jax.random.key(seed), 6)
    return {
        "inputs": noise_with(seeds[0], (SEQS, SEQ_LEN, D), 1.0, 6.0, ((0, 4), (1, 8)), (1, 2, 8, 2.0)),
        "queries": draw_queries(jax.random.fold_in(seeds[5], 71), 0),
        "w_kv": scatter_about(seeds[2], (D, 2 * KW), D ** -0.5, 0.09375, ((0, 16),)),
        "tile_mask": draw_tile_mask(jax.random.fold_in(seeds[5], 71), 0),
        "grad_out": scatter_about(seeds[4], (SEQS, SEQ_LEN, QW), 1.0, 6.0, ((0, 4), (1, 8))),
    }


def block_allowed(mask_rows, tok_rows):
    query_count = tok_rows // BLOCK
    reach_cols = mask_rows.shape[1]
    window_count = (REACH + 1) * query_count
    query_blk = jnp.arange(query_count, dtype=jnp.int32)[:, None]
    window_blk = jnp.arange(window_count, dtype=jnp.int32)[None, :]
    shard_back = REACH - window_blk // query_count
    key_blk = window_blk % query_count
    tile_offset = query_blk - key_blk + shard_back * query_count
    columns = jnp.arange(reach_cols, dtype=jnp.int32)
    one_hot = (columns[None, None, :] == (tile_offset - 1)[:, :, None]).astype(jnp.int32)
    tile_flag = lax.optimization_barrier(jnp.sum(mask_rows[:, None, :] * one_hot, axis=2))
    full_tiles = (tile_offset >= 1) & (tile_offset <= reach_cols) & (tile_flag > 0)
    diag_tiles = tile_offset == 0
    shape_four = (query_count, BLOCK, window_count, BLOCK)
    full_tok = jnp.broadcast_to(full_tiles[:, None, :, None], shape_four).reshape(tok_rows, window_count * BLOCK)
    diag_tok = jnp.broadcast_to(diag_tiles[:, None, :, None], shape_four).reshape(tok_rows, window_count * BLOCK)
    query_pos = (jnp.arange(tok_rows, dtype=jnp.int32) % BLOCK)[:, None]
    key_pos = (jnp.arange(window_count * BLOCK, dtype=jnp.int32) % BLOCK)[None, :]
    return full_tok | diag_tok & (key_pos <= query_pos)

def attend(query_rows, window, grad_rows, allowed):
    tok_rows = query_rows.shape[0]
    win_rows = window.shape[0]
    key_width = window.shape[1] // 2
    groups = HEADS // KV_HEADS
    score_scale = 1.0 / math.sqrt(HEAD_DIM)
    query_heads = query_rows.astype(jnp.float32).reshape(tok_rows, KV_HEADS, groups, HEAD_DIM)
    key_heads = window[:, :key_width].astype(jnp.float32).reshape(win_rows, KV_HEADS, HEAD_DIM)
    value_heads = window[:, key_width:].astype(jnp.float32).reshape(win_rows, KV_HEADS, HEAD_DIM)
    grad_heads = grad_rows.astype(jnp.float32).reshape(tok_rows, KV_HEADS, groups, HEAD_DIM)
    scores = jnp.einsum('tkgd,wkd->kgtw', query_heads, key_heads) * score_scale
    scores = jnp.where(allowed, scores, -jnp.inf)
    row_top = lax.optimization_barrier(jnp.max(scores, axis=-1, keepdims=True))
    weights = jnp.where(allowed, jnp.exp(scores - row_top), 0.0)
    prob_share = weights / lax.optimization_barrier(jnp.sum(weights, axis=-1, keepdims=True))
    prob_bf16 = prob_share.astype(jnp.bfloat16)
    attended = jnp.einsum('kgtw,wkd->tkgd', prob_bf16.astype(jnp.float32), value_heads).astype(jnp.bfloat16)
    grad_prob = jnp.einsum('tkgd,wkd->kgtw', grad_heads, value_heads)
    row_delta = jnp.einsum('tkgd,tkgd->kgt', grad_heads, attended.astype(jnp.float32))[..., None]
    grad_score = (prob_share * (grad_prob - row_delta) * score_scale).astype(jnp.bfloat16)
    grad_score_f = grad_score.astype(jnp.float32)
    grad_query = jnp.einsum('kgtw,wkd->tkgd', grad_score_f, key_heads).astype(jnp.bfloat16)
    grad_key = jnp.einsum('kgtw,tkgd->wkd', grad_score_f, query_heads)
    grad_value = jnp.einsum('kgtw,tkgd->wkd', prob_bf16.astype(jnp.float32), grad_heads)
    grad_window = jnp.concatenate([grad_key.reshape(win_rows, key_width), grad_value.reshape(win_rows, key_width)], axis=1)
    return (attended.reshape(tok_rows, -1), grad_query.reshape(tok_rows, -1), grad_window)

def reference(inputs, queries, w_kv, tile_mask, grad_out):
    seq_count = inputs.shape[0]
    seq_length = inputs.shape[1]
    shard_count = seq_length // TOK
    query_count = TOK // BLOCK
    pair_width = w_kv.shape[1]
    grad_total = jnp.zeros((inputs.shape[2], pair_width), jnp.float32)
    attended_all = []
    grad_q_all = []
    grad_in_all = []
    for seq_index in range(seq_count):
        key_vals = jnp.dot(inputs[seq_index], w_kv, preferred_element_type=jnp.float32).astype(jnp.bfloat16)
        padded = jnp.concatenate([jnp.zeros((REACH * TOK, pair_width), jnp.bfloat16), key_vals], axis=0)
        seq_queries = queries[seq_index]
        seq_grads = grad_out[seq_index]

        def shard_step(running, shard):
            start = (shard * TOK).astype(jnp.int32)
            window = lax.dynamic_slice_in_dim(padded, start, (REACH + 1) * TOK, 0)
            query_rows = lax.dynamic_slice_in_dim(seq_queries, start, TOK, 0)
            grad_rows = lax.dynamic_slice_in_dim(seq_grads, start, TOK, 0)
            mask_rows = lax.dynamic_slice_in_dim(tile_mask, (shard * query_count).astype(jnp.int32), query_count, 0)
            allowed = block_allowed(mask_rows, TOK)
            attended, grad_query, grad_window = attend(query_rows, window, grad_rows, allowed)
            updated = lax.dynamic_slice_in_dim(running, start, (REACH + 1) * TOK, 0) + grad_window
            running = lax.dynamic_update_slice_in_dim(running, updated, start, 0)
            return (running, (attended, grad_query))
        running = jnp.zeros(((shard_count + REACH) * TOK, pair_width), jnp.float32)
        running, (attended, grad_query) = lax.scan(shard_step, running, jnp.arange(shard_count, dtype=jnp.int32))
        grad_kv = running[REACH * TOK:].astype(jnp.bfloat16)
        grad_in = lax.dot_general(grad_kv, w_kv, (((1,), (1,)), ((), ())), preferred_element_type=jnp.float32)
        grad_in_all.append(grad_in.astype(jnp.bfloat16))
        grad_total = grad_total + lax.dot_general(inputs[seq_index], grad_kv, (((0,), (0,)), ((), ())), preferred_element_type=jnp.float32)
        attended_all.append(attended.reshape(seq_length, -1))
        grad_q_all.append(grad_query.reshape(seq_length, -1))
    grad_weights = grad_total / math.sqrt(seq_count * seq_length)
    return (jnp.stack(attended_all), jnp.stack(grad_q_all), jnp.stack(grad_in_all), grad_weights)
```

```python
import functools
import math

import jax
import jax.numpy as jnp
from jax import lax
from jax.experimental import pallas as pl
from jax.experimental.pallas import tpu as pltpu
from jax.sharding import PartitionSpec as P

HEADS = 32
KV_HEADS = 4
HEAD_DIM = 128
BLOCK = 128
REACH = 4
GROUPS = HEADS // KV_HEADS
INNER = 2

NT = (((1,), (1,)), ((), ()))
NN = (((1,), (0,)), ((), ()))
TN = (((0,), (0,)), ((), ()))


def dot(a, b, dims):
    return lax.dot_general(a, b, dims, preferred_element_type=jnp.float32)


def attend_kernel(flags, q_ref, g_ref, *refs):
    pieces = refs[: REACH + 1]
    o_ref, dq_ref, far_ref, near_ref, bias, acc_k, acc_v = refs[REACH + 1 :]
    tok = q_ref.shape[0]
    scale = 1.0 / math.sqrt(HEAD_DIM)
    scale_log2 = scale * math.log2(math.e)

    @pl.when(pl.program_id(0) == 0)
    def _():
        row = lax.broadcasted_iota(jnp.int32, (2 * tok, BLOCK), 0) % tok
        col = lax.broadcasted_iota(jnp.int32, (2 * tok, BLOCK), 1)
        for j in range(REACH):
            flag = jnp.full((2 * tok, BLOCK), flags[0, REACH - 1 - j], jnp.int32)
            bias[:, j * BLOCK : (j + 1) * BLOCK] = jnp.where(flag > 0, 0.0, -jnp.inf)
        bias[:, REACH * BLOCK :] = jnp.where(col <= row, 0.0, -jnp.inf)

    k = jnp.concatenate([p[0] for p in pieces], axis=0)
    v = jnp.concatenate([p[1] for p in pieces], axis=0)
    pairs = GROUPS // 2
    for p in range(pairs):
        lo = slice(2 * p * HEAD_DIM, (2 * p + 1) * HEAD_DIM)
        hi = slice((2 * p + 1) * HEAD_DIM, (2 * p + 2) * HEAD_DIM)
        q2 = jnp.concatenate([q_ref[:, lo], q_ref[:, hi]], axis=0)
        g2 = jnp.concatenate([g_ref[:, lo], g_ref[:, hi]], axis=0)
        s = dot(q2, k, NT) * scale_log2 + bias[...]
        top = jnp.max(s, axis=1, keepdims=True)
        e = jnp.exp2(s - top)
        share = e * (1.0 / jnp.sum(e, axis=1, keepdims=True))
        prob = share.astype(jnp.bfloat16)
        o = dot(prob, v, NN).astype(jnp.bfloat16)
        o_ref[:, lo] = o[:tok]
        o_ref[:, hi] = o[tok:]
        delta = jnp.sum(g2.astype(jnp.float32) * o.astype(jnp.float32), axis=1, keepdims=True)
        dp = dot(g2, v, NT)
        ds = (share * ((dp - delta) * scale)).astype(jnp.bfloat16)
        dq = dot(ds, k, NN).astype(jnp.bfloat16)
        dq_ref[:, lo] = dq[:tok]
        dq_ref[:, hi] = dq[tok:]
        part_k = dot(q2, ds, TN)
        part_v = dot(g2, prob, TN)
        if p == 0:
            acc_k[...] = part_k
            acc_v[...] = part_v
        elif p < pairs - 1:
            acc_k[...] += part_k
            acc_v[...] += part_v
        else:
            for slot, total in ((0, (acc_k[...] + part_k).T), (1, (acc_v[...] + part_v).T)):
                for j in range(REACH):
                    far_ref[j, slot] = total[j * BLOCK : (j + 1) * BLOCK].astype(jnp.bfloat16)
                near_ref[slot] = total[REACH * BLOCK :]


def attend(queries, grads, pieces, flags):
    tok = queries.shape[0]
    key_width = pieces[0].shape[2]
    wide = pl.BlockSpec((tok, GROUPS * HEAD_DIM), lambda i: (0, i))
    piece = pl.BlockSpec((2, tok, HEAD_DIM), lambda i: (0, 0, i))
    win = (REACH + 1) * tok
    return pl.pallas_call(
        attend_kernel,
        grid=(key_width // HEAD_DIM,),
        in_specs=[pl.BlockSpec(memory_space=pltpu.SMEM), wide, wide] + [piece] * (REACH + 1),
        out_specs=[wide, wide, pl.BlockSpec((REACH, 2, tok, HEAD_DIM), lambda i: (0, 0, 0, i)), piece],
        out_shape=[
            jax.ShapeDtypeStruct(queries.shape, jnp.bfloat16),
            jax.ShapeDtypeStruct(queries.shape, jnp.bfloat16),
            jax.ShapeDtypeStruct((REACH, 2, tok, key_width), jnp.bfloat16),
            jax.ShapeDtypeStruct((2, tok, key_width), jnp.float32),
        ],
        scratch_shapes=[
            pltpu.VMEM((2 * tok, win), jnp.float32),
            pltpu.VMEM((HEAD_DIM, win), jnp.float32),
            pltpu.VMEM((HEAD_DIM, win), jnp.float32),
        ],
        compiler_params=pltpu.CompilerParams(vmem_limit_bytes=40 << 20),
        name="attend",
    )(flags, queries, grads, *pieces)


def along(x, by):
    peers = lax.axis_size("ctx")
    return lax.ppermute(x, "ctx", [(i, i + by) for i in range(peers) if 0 <= i + by < peers])


def outer_shift(x, by):
    peers = lax.axis_size("ctx")
    return lax.ppermute(x, "ctx", [(i, (i + INNER * by) % peers) for i in range(peers)])


def swap_inner(x):
    return lax.ppermute(x, "ctx", [(i, i ^ 1) for i in range(lax.axis_size("ctx"))])


def swap_fsdp(x):
    return lax.ppermute(x, "fsdp", [(0, 1), (1, 0)])


def swap_core(x):
    return lax.ppermute(x, "dp", [(0, 1), (1, 0)])


def part(x, index, size, axis):
    return lax.dynamic_slice_in_dim(x, index * size, size, axis)


def per_device(inputs, queries, w_kv, tile_mask, grad_out):
    rows_in = inputs[0]
    tok, width = rows_in.shape
    rows, pair_width = w_kv.shape
    half = pair_width // 2
    ctx, fsdp, core = (lax.axis_index(a) for a in ("ctx", "fsdp", "dp"))
    outer = lax.axis_size("ctx") // INNER
    z, x = ctx // INNER, ctx % INNER

    own = part(w_kv, core, half, 1)
    cols = [own] + [outer_shift(own, r) for r in range(1, outer)]
    rows_both = jnp.concatenate([rows_in, swap_core(rows_in)], axis=0)
    kv_sum = None
    weights = []
    for r, col in enumerate(cols):
        by_x, by_y = swap_inner(col), swap_fsdp(col)
        diag_top = swap_fsdp(by_x[: rows // 2])
        diag_bottom = swap_inner(by_y[rows // 2 :])
        blocks = jnp.concatenate([col, by_y, by_x, diag_top, diag_bottom], axis=0)
        weights.append(blocks)
        zr = (z - r) % outer
        lhs = jnp.concatenate(
            [
                part(rows_both, (zr * INNER + (x ^ a)) * 2 + (fsdp ^ b), rows, 1)
                for a in range(2)
                for b in range(2)
            ],
            axis=1,
        )
        term = dot(lhs, blocks, NN)
        kv_sum = term if kv_sum is None else kv_sum + term
    kv = kv_sum.astype(jnp.bfloat16)
    mine, theirs = kv[:tok], swap_core(kv[tok:])
    key_vals = jnp.where(core == 0, jnp.stack([mine, theirs]), jnp.stack([theirs, mine]))
    weight_half = jnp.concatenate(weights, axis=0)
    weight_other = swap_core(weight_half)

    pieces = [along(key_vals, s) for s in range(REACH, 0, -1)] + [key_vals]
    attended, grad_query, far, near = attend(queries[0], grad_out[0], pieces, tile_mask)
    total = near
    for s in range(1, REACH + 1):
        total = total + along(far[REACH - s], -s).astype(jnp.float32)
    grad_kv = total.astype(jnp.bfloat16)
    grad_mine = jnp.where(core == 0, grad_kv[0], grad_kv[1])
    grad_theirs = jnp.where(core == 0, grad_kv[1], grad_kv[0])

    grad_rel = (dot(grad_mine, weight_half, NT) + dot(grad_theirs, weight_other, NT)).astype(
        jnp.bfloat16
    )
    spots = [
        ((z - zz) % outer * INNER + (x ^ xx)) * 2 + (fsdp ^ yy)
        for zz in range(outer)
        for xx in range(2)
        for yy in range(2)
    ]
    grad_in = jnp.concatenate([part(grad_rel, s, rows, 1) for s in spots], axis=1)

    block = width // outer
    in_cols = [part(rows_in, z, block, 1)] + [
        outer_shift(part(rows_in, (z + r) % outer, block, 1), r) for r in range(1, outer)
    ]
    in_mine = jnp.stack(in_cols)
    in_other = swap_core(in_mine)
    grad_pair = jnp.concatenate([grad_mine, swap_core(grad_theirs)], axis=0)
    tile = None
    for r in range(outer):
        gathered = grad_pair if r == 0 else outer_shift(grad_pair, r)
        term = dot(jnp.concatenate([in_mine[r], in_other[r]], axis=0), gathered, TN)
        tile = term if tile is None else tile + term
    tile = tile.reshape(2, 2, rows, half)
    first, second = tile[..., : half // 2], tile[..., half // 2 :]

    def pick(t, index, axis):
        return lax.dynamic_index_in_dim(t, index, axis, keepdims=False)

    def sent(t, swap):
        return swap(t.astype(jnp.bfloat16)).astype(jnp.float32)

    first = pick(first, x, 0) + sent(pick(first, 1 - x, 0), swap_inner)
    second = pick(second, fsdp, 1) + sent(pick(second, 1 - fsdp, 1), swap_fsdp)
    first = pick(first, fsdp, 0) + sent(pick(first, 1 - fsdp, 0), swap_fsdp)
    second = pick(second, x, 0) + sent(pick(second, 1 - x, 0), swap_inner)
    tokens = lax.axis_size("fsdp") * lax.axis_size("dp") * lax.axis_size("ctx") * tok
    grad_half = jnp.concatenate([first, second], axis=1) * (1.0 / math.sqrt(tokens))
    grad_rest = swap_core(grad_half)
    weight_grad = jnp.where(
        core == 0,
        jnp.concatenate([grad_half, grad_rest], axis=1),
        jnp.concatenate([grad_rest, grad_half], axis=1),
    )
    return (attended[None], grad_query[None], grad_in[None], weight_grad)


def solution(mesh):
    return jax.shard_map(
        per_device,
        mesh=mesh,
        in_specs=(
            P(("fsdp", "dp"), "ctx", None),
            P(("fsdp", "dp"), "ctx", None),
            P(("ctx", "fsdp"), None),
            P("ctx", None),
            P(("fsdp", "dp"), "ctx", None),
        ),
        out_specs=(
            P(("fsdp", "dp"), "ctx", None),
            P(("fsdp", "dp"), "ctx", None),
            P(("fsdp", "dp"), "ctx", None),
            P(("ctx", "fsdp"), None),
        ),
        check_vma=False,
    )
```

```python
import functools
import math

import jax
import jax.numpy as jnp
from jax import lax
from jax.experimental import pallas as pl
from jax.experimental.pallas import tpu as pltpu
from jax.sharding import PartitionSpec as P

HEADS = 32
KV_HEADS = 4
HEAD_DIM = 128
BLOCK = 128
REACH = 4
GROUPS = HEADS // KV_HEADS
INNER = 2

NT = (((1,), (1,)), ((), ()))
NN = (((1,), (0,)), ((), ()))
TN = (((0,), (0,)), ((), ()))


def dot(a, b, dims):
    return lax.dot_general(a, b, dims, preferred_element_type=jnp.float32)


def project_kernel(count, spots, mine_ref, theirs_ref, *refs):
    blocks = refs[:count]
    carry = refs[count] if len(refs) > count + 6 else None
    out_ref, lhs, total, rhs, lhs_sems, rhs_sems = refs[-6:]
    tok = mine_ref.shape[0]
    groups, _, group = lhs.shape
    unit = rhs.shape[2]
    copies, fetches = [], []
    for g in range(groups):
        at = pl.ds(pl.multiple_of(spots[g, 0] * group, group), group)
        for i, src in enumerate((mine_ref, theirs_ref)):
            rows = pl.ds(i * tok, tok)
            copies.append(
                pltpu.make_async_copy(src.at[:, at], lhs.at[g, rows, :], lhs_sems.at[g, i])
            )
            copies[-1].start()
        for kind in range(4):
            j = 4 * g + kind
            fetches.append(pltpu.make_async_copy(blocks[j], rhs.at[g, kind], rhs_sems.at[j]))
            fetches[-1].start()
    if carry is None:
        total[...] = jnp.zeros_like(total)
    else:
        total[...] = carry[...]
    for g in range(groups):
        copies[2 * g].wait()
        copies[2 * g + 1].wait()
        for kind in range(4):
            fetches[4 * g + kind].wait()
            at = pl.ds(pl.multiple_of(spots[g, 1 + kind] * unit, unit), unit)
            total[...] += dot(lhs[g, :, at], rhs[g, kind], NN)
    out_ref[...] = total[...].astype(out_ref.dtype)


def project(spots, mine, theirs, blocks, carry, out_type):
    vmem = pl.BlockSpec(memory_space=pltpu.VMEM)
    hbm = pl.BlockSpec(memory_space=pltpu.HBM)
    extra = [] if carry is None else [carry]
    tok = mine.shape[0]
    rows, half = blocks[0].shape
    groups = len(blocks) // 4
    return pl.pallas_call(
        functools.partial(project_kernel, len(blocks)),
        in_specs=[pl.BlockSpec(memory_space=pltpu.SMEM)]
        + [hbm] * (2 + len(blocks))
        + [vmem] * len(extra),
        out_specs=vmem,
        out_shape=jax.ShapeDtypeStruct((2 * tok, half), out_type),
        scratch_shapes=[
            pltpu.VMEM((groups, 2 * tok, 4 * rows), mine.dtype),
            pltpu.VMEM((2 * tok, half), jnp.float32),
            pltpu.VMEM((groups, 4, rows, half), mine.dtype),
            pltpu.SemaphoreType.DMA((groups, 2)),
            pltpu.SemaphoreType.DMA((len(blocks),)),
        ],
        compiler_params=pltpu.CompilerParams(vmem_limit_bytes=16 << 20),
        name="project",
    )(spots, mine, theirs, *blocks, *extra)


def assemble_kernel(spots, *refs):
    blocks = refs[:-4]
    out_ref, held, sems, out_sem = refs[-4:]
    unit = blocks[0].shape[0]
    copies = []
    for j, block in enumerate(blocks):
        at = pl.ds(pl.multiple_of(spots[j] * unit, unit), unit)
        copies.append(pltpu.make_async_copy(block, held.at[at, :], sems.at[j]))
        copies[-1].start()
    for copy in copies:
        copy.wait()
    write = pltpu.make_async_copy(held, out_ref, out_sem)
    write.start()
    write.wait()


def assemble(spots, blocks):
    hbm = pl.BlockSpec(memory_space=pltpu.HBM)
    rows = sum(b.shape[0] for b in blocks)
    shape = (rows, blocks[0].shape[1])
    return pl.pallas_call(
        assemble_kernel,
        in_specs=[pl.BlockSpec(memory_space=pltpu.SMEM)] + [hbm] * len(blocks),
        out_specs=hbm,
        out_shape=jax.ShapeDtypeStruct(shape, blocks[0].dtype),
        scratch_shapes=[
            pltpu.VMEM(shape, blocks[0].dtype),
            pltpu.SemaphoreType.DMA((len(blocks),)),
            pltpu.SemaphoreType.DMA,
        ],
        compiler_params=pltpu.CompilerParams(vmem_limit_bytes=16 << 20),
        name="assemble",
    )(spots, *blocks)


def attend_kernel(inner, flags, q_ref, g_ref, *refs):
    c_ref, b_ref, e_ref, a_ref, d_ref, own_ref = refs[:6]
    o_ref, dq_ref, far_c, far_be, far_a, far_d, near, bias, acc_k, acc_v = refs[6:]
    tok = q_ref.shape[0]
    scale = 1.0 / math.sqrt(HEAD_DIM)
    scale_log2 = scale * math.log2(math.e)
    even = inner[0] == 0

    @pl.when(pl.program_id(0) == 0)
    def _():
        row = lax.broadcasted_iota(jnp.int32, (2 * tok, BLOCK), 0) % tok
        col = lax.broadcasted_iota(jnp.int32, (2 * tok, BLOCK), 1)
        backs = (
            flags[0, 3],
            jnp.where(even, flags[0, 2], flags[0, 0]),
            flags[0, 1],
            jnp.where(even, flags[0, 0], flags[0, 2]),
        )
        for j, back in enumerate(backs):
            flag = jnp.full((2 * tok, BLOCK), back, jnp.int32)
            bias[:, j * BLOCK : (j + 1) * BLOCK] = jnp.where(flag > 0, 0.0, -jnp.inf)
        bias[:, REACH * BLOCK :] = jnp.where(col <= row, 0.0, -jnp.inf)

    def window(slot):
        either = jnp.where(even, e_ref[slot], b_ref[slot])
        return jnp.concatenate(
            [c_ref[slot], either, a_ref[slot], d_ref[slot], own_ref[slot]], axis=0
        )

    k, v = window(0), window(1)
    pairs = GROUPS // 2
    for p in range(pairs):
        lo = slice(2 * p * HEAD_DIM, (2 * p + 1) * HEAD_DIM)
        hi = slice((2 * p + 1) * HEAD_DIM, (2 * p + 2) * HEAD_DIM)
        q2 = jnp.concatenate([q_ref[:, lo], q_ref[:, hi]], axis=0)
        g2 = jnp.concatenate([g_ref[:, lo], g_ref[:, hi]], axis=0)
        s = dot(q2, k, NT) * scale_log2 + bias[...]
        top = jnp.max(s, axis=1, keepdims=True)
        e = jnp.exp2(s - top)
        share = e * (1.0 / jnp.sum(e, axis=1, keepdims=True))
        prob = share.astype(jnp.bfloat16)
        o = dot(prob, v, NN).astype(jnp.bfloat16)
        o_ref[:, lo] = o[:tok]
        o_ref[:, hi] = o[tok:]
        delta = jnp.sum(g2.astype(jnp.float32) * o.astype(jnp.float32), axis=1, keepdims=True)
        dp = dot(g2, v, NT)
        ds = (share * ((dp - delta) * scale)).astype(jnp.bfloat16)
        dq = dot(ds, k, NN).astype(jnp.bfloat16)
        dq_ref[:, lo] = dq[:tok]
        dq_ref[:, hi] = dq[tok:]
        part_k = dot(q2, ds, TN)
        part_v = dot(g2, prob, TN)
        if p == 0:
            acc_k[...] = part_k
            acc_v[...] = part_v
        elif p < pairs - 1:
            acc_k[...] += part_k
            acc_v[...] += part_v
        else:
            for slot, total in ((0, (acc_k[...] + part_k).T), (1, (acc_v[...] + part_v).T)):
                for j, ref in enumerate((far_c, far_be, far_a, far_d, near)):
                    ref[slot] = total[j * BLOCK : (j + 1) * BLOCK].astype(ref.dtype)


def attend(queries, grads, pieces, flags, inner):
    tok = queries.shape[0]
    key_width = pieces[0].shape[2]
    wide = pl.BlockSpec((tok, GROUPS * HEAD_DIM), lambda i: (0, i))
    piece = pl.BlockSpec((2, tok, HEAD_DIM), lambda i: (0, 0, i))
    smem = pl.BlockSpec(memory_space=pltpu.SMEM)
    win = (REACH + 1) * tok
    types = [jnp.float32, jnp.bfloat16, jnp.float32, jnp.bfloat16, jnp.float32]
    return pl.pallas_call(
        attend_kernel,
        grid=(key_width // HEAD_DIM,),
        in_specs=[smem, smem, wide, wide] + [piece] * 6,
        out_specs=[wide, wide] + [piece] * 5,
        out_shape=[jax.ShapeDtypeStruct(queries.shape, jnp.bfloat16)] * 2
        + [jax.ShapeDtypeStruct((2, tok, key_width), t) for t in types],
        scratch_shapes=[
            pltpu.VMEM((2 * tok, win), jnp.float32),
            pltpu.VMEM((HEAD_DIM, win), jnp.float32),
            pltpu.VMEM((HEAD_DIM, win), jnp.float32),
        ],
        compiler_params=pltpu.CompilerParams(vmem_limit_bytes=16 << 20),
        name="attend",
    )(inner, flags, queries, grads, *pieces)


def outer_step(x, by):
    peers = lax.axis_size("ctx")
    by = by * INNER
    return lax.ppermute(x, "ctx", [(i, i + by) for i in range(peers) if 0 <= i + by < peers])


def to_inner(x, place):
    peers = lax.axis_size("ctx")
    return lax.ppermute(x, "ctx", [(i ^ 1, i) for i in range(peers) if i % INNER == place])


def outer_shift(x, by):
    peers = lax.axis_size("ctx")
    return lax.ppermute(x, "ctx", [(i, (i + INNER * by) % peers) for i in range(peers)])


def swap_inner(x):
    return lax.ppermute(x, "ctx", [(i, i ^ 1) for i in range(lax.axis_size("ctx"))])


def swap_fsdp(x):
    return lax.ppermute(x, "fsdp", [(0, 1), (1, 0)])


def swap_core(x):
    return lax.ppermute(x, "dp", [(0, 1), (1, 0)])


def part(x, index, size, axis):
    return lax.dynamic_slice_in_dim(x, index * size, size, axis)


def per_device(inputs, queries, w_kv, tile_mask, grad_out):
    rows_in = inputs[0]
    tok, width = rows_in.shape
    rows, pair_width = w_kv.shape
    half = pair_width // 2
    ctx, fsdp, core = (lax.axis_index(a) for a in ("ctx", "fsdp", "dp"))
    outer = lax.axis_size("ctx") // INNER
    z, x = ctx // INNER, ctx % INNER
    order = list(range(outer))
    late, early = order[-1:], order[:-1]

    plane = [(x ^ i) * 2 + (fsdp ^ j) for i, j in ((0, 0), (1, 0), (0, 1), (1, 1))]
    spots = {r: [(z - r) % outer] + plane for r in order}

    def places(which):
        return jnp.stack([v for r in which for v in spots[r]]).astype(jnp.int32).reshape(-1, 5)

    known = {
        "early": places(early or late),
        "late": places(late),
        "flat": jnp.stack([spots[r][0] * 4 + v for r in order for v in plane]).astype(jnp.int32),
        "inner": x.reshape(1).astype(jnp.int32),
        "to": [((z + r) % outer) * (width // outer) for r in range(outer)],
        "half": core * half,
        "first": core == 0,
        "x": x,
        "not_x": 1 - x,
        "even": x == 0,
        "y": fsdp,
        "not_y": 1 - fsdp,
    }
    for k in ("half", "x", "not_x", "y", "not_y"):
        known[k] = known[k].astype(jnp.uint32)
    known["to"] = [t.astype(jnp.uint32) for t in known["to"]]
    known, w_kv = lax.optimization_barrier((known, w_kv))
    x, not_x, even, y, not_y, first_core = (
        known[k] for k in ("x", "not_x", "even", "y", "not_y", "first")
    )

    own = lax.dynamic_slice_in_dim(w_kv, known["half"], half, 1)
    cols = [own]
    for r in range(1, outer):
        cols.append(outer_shift(cols[-1], 1))
    theirs_in = swap_core(rows_in)
    blocks = {}
    for r in order:
        col = cols[r]
        by_x, by_y = swap_inner(col), swap_fsdp(col)
        blocks[r] = [col, by_x, by_y, swap_fsdp(by_x) if r % 2 == 0 else swap_inner(by_y)]

    def listed(which):
        return [v for r in which for v in blocks[r]]

    by_blocks = rows % 128 == 0
    if by_blocks:
        part_sum = project(known["early"], rows_in, theirs_in, listed(early), None, jnp.float32)
        kv = project(known["late"], rows_in, theirs_in, listed(late), part_sum, jnp.bfloat16)
    else:
        weight_half = jnp.zeros((width, half), w_kv.dtype)
        for i, block in enumerate(listed(order)):
            at = known["flat"][i] * rows
            weight_half = lax.dynamic_update_slice_in_dim(weight_half, block, at, 0)
        kv = dot(jnp.concatenate([rows_in, theirs_in], axis=0), weight_half, NN).astype(jnp.bfloat16)
    block = width // outer
    held_in = lax.optimization_barrier((rows_in, cols[-1]))[0]

    def columns(t, r):
        return lax.dynamic_slice_in_dim(t, known["to"][r], block, 1)

    in_mine = [outer_shift(columns(held_in, r), r) for r in range(1, outer)]
    kv, *in_mine = lax.optimization_barrier((kv, *in_mine))
    in_theirs = [columns(theirs_in, 0)] + [swap_core(t) for t in in_mine]
    in_mine = [columns(rows_in, 0)] + in_mine

    mine, theirs = kv[:tok], swap_core(kv[tok:])
    key_vals = jnp.where(first_core, jnp.stack([mine, theirs]), jnp.stack([theirs, mine]))

    back_a = outer_step(key_vals, 1)
    back_b = to_inner(key_vals, 1)
    if by_blocks:
        tied = lax.optimization_barrier((*listed(order), kv))
        weight_half = assemble(known["flat"], list(tied[:-1]))
        weight_half, back_a = lax.optimization_barrier((weight_half, back_a))
    back_c = outer_step(back_a, 1)
    back_d = swap_inner(back_a)
    back_e = to_inner(back_c, 0)
    weight_other = swap_core(weight_half)

    queries, in_theirs = lax.optimization_barrier((queries, in_theirs))
    attended, grad_query, far_c, far_be, far_a, far_d, near = attend(
        queries[0],
        grad_out[0],
        [back_c, back_b, back_e, back_a, back_d, key_vals],
        tile_mask,
        known["inner"],
    )
    got_be = swap_inner(far_be).astype(jnp.float32)
    got_d = swap_inner(far_d).astype(jnp.float32)
    sent_c = (far_c + jnp.where(even, 0.0, got_be)).astype(jnp.bfloat16)
    got_c = outer_step(sent_c, -1).astype(jnp.float32)
    sent_a = (far_a + got_d + got_c).astype(jnp.bfloat16)
    got_a = outer_step(sent_a, -1).astype(jnp.float32)
    grad_kv = (near + jnp.where(even, got_be, 0.0) + got_a).astype(jnp.bfloat16)
    grad_mine = jnp.where(first_core, grad_kv[0], grad_kv[1])
    grad_theirs = jnp.where(first_core, grad_kv[1], grad_kv[0])

    grad_in = (dot(grad_mine, weight_half, NT) + dot(grad_theirs, weight_other, NT)).astype(
        jnp.bfloat16
    )

    grad_pair = jnp.concatenate([grad_mine, swap_core(grad_theirs)], axis=0)
    tile = None
    for r in range(outer):
        gathered = grad_pair if r == 0 else outer_shift(grad_pair, r)
        if r == min(1, outer - 1):
            gathered, grad_in = lax.optimization_barrier((gathered, grad_in))
        term = dot(jnp.concatenate([in_mine[r], in_theirs[r]], axis=0), gathered, TN)
        tile = term if tile is None else tile + term
    tile = tile.reshape(2, 2, rows, half)
    first, second = tile[..., : half // 2], tile[..., half // 2 :]

    def pick(t, index, axis):
        return lax.dynamic_index_in_dim(t, index, axis, keepdims=False)

    def sent(t, swap):
        return swap(t.astype(jnp.bfloat16)).astype(jnp.float32)

    first = pick(first, x, 0) + sent(pick(first, not_x, 0), swap_inner)
    second = pick(second, y, 1) + sent(pick(second, not_y, 1), swap_fsdp)
    first = pick(first, y, 0) + sent(pick(first, not_y, 0), swap_fsdp)
    second = pick(second, x, 0) + sent(pick(second, not_x, 0), swap_inner)
    tokens = lax.axis_size("fsdp") * lax.axis_size("dp") * lax.axis_size("ctx") * tok
    grad_half = jnp.concatenate([first, second], axis=1) * (1.0 / math.sqrt(tokens))
    grad_rest = swap_core(grad_half)
    weight_grad = jnp.where(
        first_core,
        jnp.concatenate([grad_half, grad_rest], axis=1),
        jnp.concatenate([grad_rest, grad_half], axis=1),
    )
    return (attended[None], grad_query[None], grad_in[None], weight_grad)


def solution(mesh):
    return jax.shard_map(
        per_device,
        mesh=mesh,
        in_specs=(
            P(("fsdp", "dp"), "ctx", None),
            P(("fsdp", "dp"), "ctx", None),
            P(("ctx", "fsdp"), None),
            P("ctx", None),
            P(("fsdp", "dp"), "ctx", None),
        ),
        out_specs=(
            P(("fsdp", "dp"), "ctx", None),
            P(("fsdp", "dp"), "ctx", None),
            P(("fsdp", "dp"), "ctx", None),
            P(("ctx", "fsdp"), None),
        ),
        check_vma=False,
    )
```

```python
import functools
import math

import jax
import jax.numpy as jnp
from jax import lax
from jax.experimental import pallas as pl
from jax.experimental.pallas import tpu as pltpu
from jax.sharding import PartitionSpec as P

HEADS = 32
KV_HEADS = 4
HEAD_DIM = 128
BLOCK = 128
REACH = 4
GROUPS = HEADS // KV_HEADS
INNER = 2
PLANE = ((0, 0), (1, 1), (1, 0), (0, 1))

NT = (((1,), (1,)), ((), ()))
NN = (((1,), (0,)), ((), ()))
TN = (((0,), (0,)), ((), ()))


def dot(a, b, dims):
    return lax.dot_general(a, b, dims, preferred_element_type=jnp.float32)


def project_kernel(count, spots, mine_ref, theirs_ref, *refs):
    blocks = refs[:count]
    carry = refs[count] if len(refs) > count + 6 else None
    out_ref, lhs, total, rhs, lhs_sems, rhs_sems = refs[-6:]
    tok = mine_ref.shape[0]
    groups, _, group = lhs.shape
    unit = rhs.shape[2]
    copies, fetches = [], []
    for g in range(groups):
        at = pl.ds(pl.multiple_of(spots[g, 0] * group, group), group)
        for i, src in enumerate((mine_ref, theirs_ref)):
            rows = pl.ds(i * tok, tok)
            copies.append(
                pltpu.make_async_copy(src.at[:, at], lhs.at[g, rows, :], lhs_sems.at[g, i])
            )
            copies[-1].start()
        for kind in range(4):
            j = 4 * g + kind
            fetches.append(pltpu.make_async_copy(blocks[j], rhs.at[g, kind], rhs_sems.at[j]))
            fetches[-1].start()
    if carry is None:
        total[...] = jnp.zeros_like(total)
    else:
        total[...] = carry[...]
    for g in range(groups):
        copies[2 * g].wait()
        copies[2 * g + 1].wait()
        for kind in range(4):
            fetches[4 * g + kind].wait()
            at = pl.ds(pl.multiple_of(spots[g, 1 + kind] * unit, unit), unit)
            total[...] += dot(lhs[g, :, at], rhs[g, kind], NN)
    out_ref[...] = total[...].astype(out_ref.dtype)


def project(spots, mine, theirs, blocks, carry, out_type):
    vmem = pl.BlockSpec(memory_space=pltpu.VMEM)
    hbm = pl.BlockSpec(memory_space=pltpu.HBM)
    extra = [] if carry is None else [carry]
    tok = mine.shape[0]
    rows, half = blocks[0].shape
    groups = len(blocks) // 4
    return pl.pallas_call(
        functools.partial(project_kernel, len(blocks)),
        in_specs=[pl.BlockSpec(memory_space=pltpu.SMEM)]
        + [hbm] * (2 + len(blocks))
        + [vmem] * len(extra),
        out_specs=vmem,
        out_shape=jax.ShapeDtypeStruct((2 * tok, half), out_type),
        scratch_shapes=[
            pltpu.VMEM((groups, 2 * tok, 4 * rows), mine.dtype),
            pltpu.VMEM((2 * tok, half), jnp.float32),
            pltpu.VMEM((groups, 4, rows, half), mine.dtype),
            pltpu.SemaphoreType.DMA((groups, 2)),
            pltpu.SemaphoreType.DMA((len(blocks),)),
        ],
        compiler_params=pltpu.CompilerParams(vmem_limit_bytes=16 << 20),
        name="project",
    )(spots, mine, theirs, *blocks, *extra)


def assemble_kernel(spots, *refs):
    blocks = refs[:-4]
    out_ref, held, sems, out_sem = refs[-4:]
    unit = blocks[0].shape[0]
    copies = []
    for j, block in enumerate(blocks):
        at = pl.ds(pl.multiple_of(spots[j] * unit, unit), unit)
        copies.append(pltpu.make_async_copy(block, held.at[at, :], sems.at[j]))
        copies[-1].start()
    for copy in copies:
        copy.wait()
    write = pltpu.make_async_copy(held, out_ref, out_sem)
    write.start()
    write.wait()


def assemble(spots, blocks):
    hbm = pl.BlockSpec(memory_space=pltpu.HBM)
    rows = sum(b.shape[0] for b in blocks)
    shape = (rows, blocks[0].shape[1])
    return pl.pallas_call(
        assemble_kernel,
        in_specs=[pl.BlockSpec(memory_space=pltpu.SMEM)] + [hbm] * len(blocks),
        out_specs=hbm,
        out_shape=jax.ShapeDtypeStruct(shape, blocks[0].dtype),
        scratch_shapes=[
            pltpu.VMEM(shape, blocks[0].dtype),
            pltpu.SemaphoreType.DMA((len(blocks),)),
            pltpu.SemaphoreType.DMA,
        ],
        compiler_params=pltpu.CompilerParams(vmem_limit_bytes=16 << 20),
        name="assemble",
    )(spots, *blocks)


def attend_kernel(inner, flags, q_ref, g_ref, *refs):
    c_ref, b_ref, e_ref, a_ref, d_ref, own_ref = refs[:6]
    o_ref, dq_ref, far_c, far_be, far_a, far_d, near, bias, acc_k, acc_v = refs[6:]
    tok = q_ref.shape[0]
    scale = 1.0 / math.sqrt(HEAD_DIM)
    scale_log2 = scale * math.log2(math.e)
    even = inner[0] == 0

    @pl.when(pl.program_id(0) == 0)
    def _():
        row = lax.broadcasted_iota(jnp.int32, (2 * tok, BLOCK), 0) % tok
        col = lax.broadcasted_iota(jnp.int32, (2 * tok, BLOCK), 1)
        backs = (
            flags[0, 3],
            jnp.where(even, flags[0, 2], flags[0, 0]),
            flags[0, 1],
            jnp.where(even, flags[0, 0], flags[0, 2]),
        )
        for j, back in enumerate(backs):
            flag = jnp.full((2 * tok, BLOCK), back, jnp.int32)
            bias[:, j * BLOCK : (j + 1) * BLOCK] = jnp.where(flag > 0, 0.0, -jnp.inf)
        bias[:, REACH * BLOCK :] = jnp.where(col <= row, 0.0, -jnp.inf)

    def window(slot):
        either = jnp.where(even, e_ref[slot], b_ref[slot])
        return jnp.concatenate(
            [c_ref[slot], either, a_ref[slot], d_ref[slot], own_ref[slot]], axis=0
        )

    k, v = window(0), window(1)
    pairs = GROUPS // 2
    for p in range(pairs):
        lo = slice(2 * p * HEAD_DIM, (2 * p + 1) * HEAD_DIM)
        hi = slice((2 * p + 1) * HEAD_DIM, (2 * p + 2) * HEAD_DIM)
        q2 = jnp.concatenate([q_ref[:, lo], q_ref[:, hi]], axis=0)
        g2 = jnp.concatenate([g_ref[:, lo], g_ref[:, hi]], axis=0)
        s = dot(q2, k, NT) * scale_log2 + bias[...]
        top = jnp.max(s, axis=1, keepdims=True)
        e = jnp.exp2(s - top)
        share = e * (1.0 / jnp.sum(e, axis=1, keepdims=True))
        prob = share.astype(jnp.bfloat16)
        o = dot(prob, v, NN).astype(jnp.bfloat16)
        o_ref[:, lo] = o[:tok]
        o_ref[:, hi] = o[tok:]
        delta = jnp.sum(g2.astype(jnp.float32) * o.astype(jnp.float32), axis=1, keepdims=True)
        dp = dot(g2, v, NT)
        ds = (share * ((dp - delta) * scale)).astype(jnp.bfloat16)
        dq = dot(ds, k, NN).astype(jnp.bfloat16)
        dq_ref[:, lo] = dq[:tok]
        dq_ref[:, hi] = dq[tok:]
        part_k = dot(q2, ds, TN)
        part_v = dot(g2, prob, TN)
        if p == 0:
            acc_k[...] = part_k
            acc_v[...] = part_v
        elif p < pairs - 1:
            acc_k[...] += part_k
            acc_v[...] += part_v
        else:
            for slot, total in ((0, (acc_k[...] + part_k).T), (1, (acc_v[...] + part_v).T)):
                for j, ref in enumerate((far_c, far_be, far_a, far_d, near)):
                    ref[slot] = total[j * BLOCK : (j + 1) * BLOCK].astype(ref.dtype)


def attend(queries, grads, pieces, flags, inner):
    tok = queries.shape[0]
    key_width = pieces[0].shape[2]
    wide = pl.BlockSpec((tok, GROUPS * HEAD_DIM), lambda i: (0, i))
    piece = pl.BlockSpec((2, tok, HEAD_DIM), lambda i: (0, 0, i))
    smem = pl.BlockSpec(memory_space=pltpu.SMEM)
    win = (REACH + 1) * tok
    types = [jnp.bfloat16, jnp.bfloat16, jnp.float32, jnp.bfloat16, jnp.float32]
    return pl.pallas_call(
        attend_kernel,
        grid=(key_width // HEAD_DIM,),
        in_specs=[smem, smem, wide, wide] + [piece] * 6,
        out_specs=[wide, wide] + [piece] * 5,
        out_shape=[jax.ShapeDtypeStruct(queries.shape, jnp.bfloat16)] * 2
        + [jax.ShapeDtypeStruct((2, tok, key_width), t) for t in types],
        scratch_shapes=[
            pltpu.VMEM((2 * tok, win), jnp.float32),
            pltpu.VMEM((HEAD_DIM, win), jnp.float32),
            pltpu.VMEM((HEAD_DIM, win), jnp.float32),
        ],
        compiler_params=pltpu.CompilerParams(vmem_limit_bytes=16 << 20),
        cost_estimate=pl.CostEstimate(
            flops=12 * queries.size * win,
            transcendentals=queries.size // HEAD_DIM * win,
            bytes_accessed=8 * queries.size + 18 * win * key_width * 2,
        ),
        name="attend",
    )(inner, flags, queries, grads, *pieces)


def outer_step(x, by):
    peers = lax.axis_size("ctx")
    by = by * INNER
    return lax.ppermute(x, "ctx", [(i, i + by) for i in range(peers) if 0 <= i + by < peers])


def to_inner(x, place):
    peers = lax.axis_size("ctx")
    return lax.ppermute(x, "ctx", [(i ^ 1, i) for i in range(peers) if i % INNER == place])


def outer_shift(x, by):
    peers = lax.axis_size("ctx")
    return lax.ppermute(x, "ctx", [(i, (i + INNER * by) % peers) for i in range(peers)])


def swap_inner(x):
    return lax.ppermute(x, "ctx", [(i, i ^ 1) for i in range(lax.axis_size("ctx"))])


def swap_fsdp(x):
    return lax.ppermute(x, "fsdp", [(0, 1), (1, 0)])


def swap_core(x):
    return lax.ppermute(x, "dp", [(0, 1), (1, 0)])


def odd_step(x, by):
    peers = lax.axis_size("ctx")
    start = 1 if by > 0 else 0
    return lax.ppermute(
        x, "ctx", [(i, i + by) for i in range(start, peers, 2) if 0 <= i + by < peers]
    )


def crossed(x, r, outer_core, plane_core=None):
    ctx, fsdp = lax.axis_size("ctx"), lax.axis_size("fsdp")
    flip_x, flip_y = PLANE[r]
    pairs = []
    for i in range(ctx):
        for j in range(fsdp):
            here = (i * fsdp + j) * 2
            if outer_core is not None:
                there = ((i + INNER * r) % ctx * fsdp + j) * 2
                pairs.append((here + outer_core, there + outer_core))
            if plane_core is not None:
                there = ((i ^ flip_x) * fsdp + (j ^ flip_y)) * 2
                pairs.append((here + plane_core, there + plane_core))
    return lax.ppermute(x, ("ctx", "fsdp", "dp"), pairs)


def split_kernel(offsets, mine_ref, theirs_ref, *refs):
    outs, held, in_sems, out_sems = refs[:4], refs[4], refs[5], refs[6]
    tok = mine_ref.shape[0]
    unit = held.shape[2] // 4
    reads = []
    for r in range(4):
        for k in range(4):
            at = pl.ds(pl.multiple_of(offsets[r, k] * unit, unit), unit)
            for i, src in enumerate((mine_ref, theirs_ref)):
                dst = held.at[r, pl.ds(i * tok, tok), pl.ds(k * unit, unit)]
                copy = pltpu.make_async_copy(src.at[:, at], dst, in_sems.at[r, k, i])
                copy.start()
                reads.append(copy)
    writes = []
    for r in range(4):
        for copy in reads[8 * r : 8 * r + 8]:
            copy.wait()
        writes.append(pltpu.make_async_copy(held.at[r], outs[r], out_sems.at[r]))
        writes[-1].start()
    for copy in writes:
        copy.wait()


def split(offsets, mine, theirs):
    hbm = pl.BlockSpec(memory_space=pltpu.HBM)
    tok, width = mine.shape
    shape = (2 * tok, width // 4)
    return pl.pallas_call(
        split_kernel,
        in_specs=[pl.BlockSpec(memory_space=pltpu.SMEM), hbm, hbm],
        out_specs=[hbm] * 4,
        out_shape=[jax.ShapeDtypeStruct(shape, mine.dtype)] * 4,
        scratch_shapes=[
            pltpu.VMEM((4,) + shape, mine.dtype),
            pltpu.SemaphoreType.DMA((4, 4, 2)),
            pltpu.SemaphoreType.DMA((4,)),
        ],
        compiler_params=pltpu.CompilerParams(vmem_limit_bytes=8 << 20),
        name="split",
    )(offsets, mine, theirs)


def per_device(inputs, queries, w_kv, tile_mask, grad_out):
    rows_in = inputs[0]
    tok, width = rows_in.shape
    rows, pair_width = w_kv.shape
    half = pair_width // 2
    ctx, fsdp, core = (lax.axis_index(a) for a in ("ctx", "fsdp", "dp"))
    outer = lax.axis_size("ctx") // INNER
    z, x = ctx // INNER, ctx % INNER
    order = list(range(outer))
    late, early = order[-1:], order[:-1]

    plane = [(x ^ i) * 2 + (fsdp ^ j) for i, j in ((0, 0), (1, 0), (0, 1), (1, 1))]
    spots = {r: [(z - r) % outer] + plane for r in order}

    def places(which):
        return jnp.stack([v for r in which for v in spots[r]]).astype(jnp.int32).reshape(-1, 5)

    mixed = outer == 4
    to_outer = [(z + r) % outer for r in range(outer)]
    to_plane = [(x ^ i) * 2 + (fsdp ^ j) for i, j in PLANE]
    cut = [jnp.where(core == 0, to_outer[r] * 4 + k, k * 4 + to_plane[r]) for r in range(4) for k in range(4)] if mixed else [x]
    known = {
        "cut": jnp.stack(cut).astype(jnp.int32).reshape(-1, 4 if mixed else 1),
        "owner": [jnp.where(core == 0, p, o).astype(jnp.uint32) for p, o in zip(to_plane, to_outer)],
        "early": places(early or late),
        "late": places(late),
        "flat": jnp.stack([spots[r][0] * 4 + v for r in order for v in plane]).astype(jnp.int32),
        "inner": x.reshape(1).astype(jnp.int32),
        "to": [((z + r) % outer) * (width // outer) for r in range(outer)],
        "half": core * half,
        "first": core == 0,
        "x": x,
        "not_x": 1 - x,
        "even": x == 0,
        "y": fsdp,
        "not_y": 1 - fsdp,
    }
    for k in ("half", "x", "not_x", "y", "not_y"):
        known[k] = known[k].astype(jnp.uint32)
    known["to"] = [t.astype(jnp.uint32) for t in known["to"]]
    known, w_kv = lax.optimization_barrier((known, w_kv))
    x, not_x, even, y, not_y, first_core = (
        known[k] for k in ("x", "not_x", "even", "y", "not_y", "first")
    )

    own = lax.dynamic_slice_in_dim(w_kv, known["half"], half, 1)
    theirs_in = swap_core(rows_in)
    tie = lax.optimization_barrier
    col, blocks, cols = own, {}, [own]
    for r in order:
        col_x = col_y = col
        if r == outer - 1 and r:
            col_x, blocks[r - 1][1] = tie((col, blocks[r - 1][1]))
            col_y, blocks[r - 1][2] = tie((col, blocks[r - 1][2]))
        following = outer_shift(col, 1) if r < outer - 1 else None
        by_x, by_y = swap_inner(col_x), swap_fsdp(col_y)
        if r == 0 and mixed:
            early_cuts = split(known["cut"], rows_in, theirs_in)
            following, by_x, by_y, early_cuts = tie((following, by_x, by_y, early_cuts))
        elif r == 1 and outer > 2:
            following, by_x = tie((following, by_x))
        blocks[r] = [col, by_x, by_y]
        col = following
        cols.append(col)
    for r in order:
        if r == 0:
            diagonal = swap_fsdp(blocks[0][1])
        elif r == outer - 1:
            diagonal = swap_inner(blocks[r][2])
        else:
            diagonal = outer_shift(diagonal, 1)
        blocks[r].append(diagonal)

    def listed(which):
        return [v for r in which for v in blocks[r]]

    by_blocks = rows % 128 == 0
    if by_blocks:
        part_sum = project(known["early"], rows_in, theirs_in, listed(early), None, jnp.float32)
        kv = project(known["late"], rows_in, theirs_in, listed(late), part_sum, jnp.bfloat16)
    else:
        weight_half = jnp.zeros((width, half), w_kv.dtype)
        for i, block in enumerate(listed(order)):
            at = known["flat"][i] * rows
            weight_half = lax.dynamic_update_slice_in_dim(weight_half, block, at, 0)
        kv = dot(jnp.concatenate([rows_in, theirs_in], axis=0), weight_half, NN).astype(jnp.bfloat16)
    block = width // outer

    def columns(t, r):
        return lax.dynamic_slice_in_dim(t, known["to"][r], block, 1)

    if mixed:
        cuts = early_cuts
    else:
        in_mine = [outer_shift(columns(rows_in, r), r) for r in range(1, outer)]
        in_theirs = [columns(theirs_in, 0)] + [swap_core(t) for t in in_mine]
        in_mine = [columns(rows_in, 0)] + in_mine

    mine, theirs = kv[:tok], swap_core(kv[tok:])
    key_vals = jnp.where(first_core, jnp.stack([mine, theirs]), jnp.stack([theirs, mine]))

    back_a = outer_step(key_vals, 1)
    back_b = to_inner(key_vals, 1)
    if by_blocks:
        tied = tie((*listed(order), kv))
        weight_half = assemble(known["flat"], list(tied[:-1]))
        weight_half, back_a = tie((weight_half, back_a))
    back_c = outer_step(back_a, 1)
    back_d = swap_inner(back_a)
    back_e = odd_step(back_a, 1)
    weight_other = swap_core(weight_half)

    if mixed:
        late_cuts, back_d = tie((cuts[1:], back_d))
        passed = [crossed(late_cuts[r - 1], r, 0, 1) for r in range(1, 4)]
    attended, grad_query, far_c, far_be, far_a, far_d, near = attend(
        queries[0],
        grad_out[0],
        [back_c, back_b, back_e, back_a, back_d, key_vals],
        tile_mask,
        known["inner"],
    )
    got_c = outer_step(far_c, -1).astype(jnp.float32)
    got_e = odd_step(far_be, -1).astype(jnp.float32)
    got_d = swap_inner(far_d).astype(jnp.float32)
    got_b = to_inner(far_be, 0).astype(jnp.float32)
    if mixed:
        far_a, passed = tie((far_a, passed))
    sent_a = (far_a + got_d + got_c + got_e).astype(jnp.bfloat16)
    got_a = outer_step(sent_a, -1).astype(jnp.float32)
    grad_kv = (near + got_b + got_a).astype(jnp.bfloat16)
    grad_mine = jnp.where(first_core, grad_kv[0], grad_kv[1])
    grad_theirs = jnp.where(first_core, grad_kv[1], grad_kv[0])

    grad_in = (dot(grad_mine, weight_half, NT) + dot(grad_theirs, weight_other, NT)).astype(
        jnp.bfloat16
    )

    grad_pair = jnp.concatenate([grad_mine, swap_core(grad_theirs)], axis=0)
    if mixed:
        in_both = [cuts[0]] + passed
    else:
        in_both = [jnp.concatenate(t, axis=0) for t in zip(in_mine, in_theirs)]
    tile = None
    for r in range(outer):
        gathered = grad_pair
        if r:
            gathered = crossed(grad_pair, r, 0, 1) if mixed else outer_shift(grad_pair, r)
        term = dot(in_both[r], gathered, TN)
        tile = term if tile is None else tile + term

    def pick(t, index, axis):
        return lax.dynamic_index_in_dim(t, index, axis, keepdims=False)

    def sent(t, swap):
        return swap(t.astype(jnp.bfloat16)).astype(jnp.float32)

    if mixed:
        tile = tile.reshape(4, rows, half)
        tile, _ = tie((tile, swap_core(tile[0, :8, :HEAD_DIM])))
        arrived = [
            crossed(pick(tile, known["owner"][r], 0).astype(jnp.bfloat16), r, 1, 0)
            for r in range(1, 4)
        ]
        arrived, grad_in = tie((arrived, grad_in))
        grad_half = pick(tile, known["owner"][0], 0)
        for t in arrived:
            grad_half += t.astype(jnp.float32)
    else:
        tile = tile.reshape(2, 2, rows, half)
        first, second = tile[..., : half // 2], tile[..., half // 2 :]
        first = pick(first, x, 0) + sent(pick(first, not_x, 0), swap_inner)
        second = pick(second, y, 1) + sent(pick(second, not_y, 1), swap_fsdp)
        first = pick(first, y, 0) + sent(pick(first, not_y, 0), swap_fsdp)
        second = pick(second, x, 0) + sent(pick(second, not_x, 0), swap_inner)
        grad_half = jnp.concatenate([first, second], axis=1)
    tokens = lax.axis_size("fsdp") * lax.axis_size("dp") * lax.axis_size("ctx") * tok
    grad_half = grad_half * (1.0 / math.sqrt(tokens))
    grad_rest = swap_core(grad_half)
    weight_grad = jnp.where(
        first_core,
        jnp.concatenate([grad_half, grad_rest], axis=1),
        jnp.concatenate([grad_rest, grad_half], axis=1),
    )
    return (attended[None], grad_query[None], grad_in[None], weight_grad)


def solution(mesh):
    return jax.shard_map(
        per_device,
        mesh=mesh,
        in_specs=(
            P(("fsdp", "dp"), "ctx", None),
            P(("fsdp", "dp"), "ctx", None),
            P(("ctx", "fsdp"), None),
            P("ctx", None),
            P(("fsdp", "dp"), "ctx", None),
        ),
        out_specs=(
            P(("fsdp", "dp"), "ctx", None),
            P(("fsdp", "dp"), "ctx", None),
            P(("fsdp", "dp"), "ctx", None),
            P(("ctx", "fsdp"), None),
        ),
        check_vma=False,
    )
```

```python
import functools
import math

import jax
import jax.numpy as jnp
from jax import lax
from jax.experimental import pallas as pl
from jax.experimental.pallas import tpu as pltpu
from jax.sharding import PartitionSpec as P

HEADS = 32
KV_HEADS = 4
HEAD_DIM = 128
BLOCK = 128
REACH = 4
GROUPS = HEADS // KV_HEADS
INNER = 2
PLANE = ((0, 0), (1, 1), (1, 0), (0, 1))

NT = (((1,), (1,)), ((), ()))
NN = (((1,), (0,)), ((), ()))
TN = (((0,), (0,)), ((), ()))


def dot(a, b, dims):
    return lax.dot_general(a, b, dims, preferred_element_type=jnp.float32)


def project_kernel(count, spots, mine_ref, theirs_ref, *refs):
    blocks = refs[:count]
    carry = refs[count] if len(refs) > count + 6 else None
    out_ref, lhs, total, rhs, lhs_sems, rhs_sems = refs[-6:]
    tok = mine_ref.shape[0]
    groups, _, group = lhs.shape
    unit = rhs.shape[2]
    copies, fetches = [], []
    for g in range(groups):
        at = pl.ds(pl.multiple_of(spots[g, 0] * group, group), group)
        for i, src in enumerate((mine_ref, theirs_ref)):
            rows = pl.ds(i * tok, tok)
            copies.append(
                pltpu.make_async_copy(src.at[:, at], lhs.at[g, rows, :], lhs_sems.at[g, i])
            )
            copies[-1].start()
        for kind in range(4):
            j = 4 * g + kind
            fetches.append(pltpu.make_async_copy(blocks[j], rhs.at[g, kind], rhs_sems.at[j]))
            fetches[-1].start()
    if carry is None:
        total[...] = jnp.zeros_like(total)
    else:
        total[...] = carry[...]
    for g in range(groups):
        copies[2 * g].wait()
        copies[2 * g + 1].wait()
        for kind in range(4):
            fetches[4 * g + kind].wait()
            at = pl.ds(pl.multiple_of(spots[g, 1 + kind] * unit, unit), unit)
            total[...] += dot(lhs[g, :, at], rhs[g, kind], NN)
    out_ref[...] = total[...].astype(out_ref.dtype)


def project(spots, mine, theirs, blocks, carry, out_type):
    vmem = pl.BlockSpec(memory_space=pltpu.VMEM)
    hbm = pl.BlockSpec(memory_space=pltpu.HBM)
    extra = [] if carry is None else [carry]
    tok = mine.shape[0]
    rows, half = blocks[0].shape
    groups = len(blocks) // 4
    return pl.pallas_call(
        functools.partial(project_kernel, len(blocks)),
        in_specs=[pl.BlockSpec(memory_space=pltpu.SMEM)]
        + [hbm] * (2 + len(blocks))
        + [vmem] * len(extra),
        out_specs=vmem,
        out_shape=jax.ShapeDtypeStruct((2 * tok, half), out_type),
        scratch_shapes=[
            pltpu.VMEM((groups, 2 * tok, 4 * rows), mine.dtype),
            pltpu.VMEM((2 * tok, half), jnp.float32),
            pltpu.VMEM((groups, 4, rows, half), mine.dtype),
            pltpu.SemaphoreType.DMA((groups, 2)),
            pltpu.SemaphoreType.DMA((len(blocks),)),
        ],
        compiler_params=pltpu.CompilerParams(vmem_limit_bytes=16 << 20),
        name="project",
    )(spots, mine, theirs, *blocks, *extra)


def assemble_kernel(spots, *refs):
    blocks = refs[:-4]
    out_ref, held, sems, out_sem = refs[-4:]
    unit = blocks[0].shape[0]
    copies = []
    for j, block in enumerate(blocks):
        at = pl.ds(pl.multiple_of(spots[j] * unit, unit), unit)
        copies.append(pltpu.make_async_copy(block, held.at[at, :], sems.at[j]))
        copies[-1].start()
    for copy in copies:
        copy.wait()
    write = pltpu.make_async_copy(held, out_ref, out_sem)
    write.start()
    write.wait()


def assemble(spots, blocks):
    hbm = pl.BlockSpec(memory_space=pltpu.HBM)
    rows = sum(b.shape[0] for b in blocks)
    shape = (rows, blocks[0].shape[1])
    return pl.pallas_call(
        assemble_kernel,
        in_specs=[pl.BlockSpec(memory_space=pltpu.SMEM)] + [hbm] * len(blocks),
        out_specs=hbm,
        out_shape=jax.ShapeDtypeStruct(shape, blocks[0].dtype),
        scratch_shapes=[
            pltpu.VMEM(shape, blocks[0].dtype),
            pltpu.SemaphoreType.DMA((len(blocks),)),
            pltpu.SemaphoreType.DMA,
        ],
        compiler_params=pltpu.CompilerParams(vmem_limit_bytes=16 << 20),
        name="assemble",
    )(spots, *blocks)


def attend_kernel(inner, flags, q_ref, g_ref, *refs):
    c_ref, b_ref, e_ref, a_ref, d_ref, own_ref = refs[:6]
    o_ref, dq_ref, far_c, far_be, far_a, far_d, near = refs[6:13]
    k_held, v_held, acc_k, acc_v = refs[13:]
    tok = q_ref.shape[0]
    scale = 1.0 / math.sqrt(HEAD_DIM)
    scale_log2 = scale * math.log2(math.e)
    even = inner[0] == 0
    backs = (
        flags[0, 3],
        jnp.where(even, flags[0, 2], flags[0, 0]),
        flags[0, 1],
        jnp.where(even, flags[0, 0], flags[0, 2]),
    )
    count, places = jnp.int32(1), []
    for back in backs:
        places.append(pl.ds(pl.multiple_of(count * BLOCK, BLOCK), BLOCK))
        count = count + jnp.where(back > 0, 1, 0)

    for slot, held in ((0, k_held), (1, v_held)):
        held[:BLOCK] = own_ref[slot]
        for j, (back, place) in enumerate(zip(backs, places)):

            @pl.when(back > 0)
            def _(slot=slot, held=held, j=j, place=place):
                if j == 1:
                    held[place, :] = jnp.where(even, e_ref[slot], b_ref[slot])
                else:
                    held[place, :] = (c_ref, None, a_ref, d_ref)[j][slot]

    def work(win):
        k, v = k_held[:win], v_held[:win]
        row = lax.broadcasted_iota(jnp.int32, (2 * tok, BLOCK), 0) % tok
        col = lax.broadcasted_iota(jnp.int32, (2 * tok, BLOCK), 1)
        seen = col <= row
        for p in range(GROUPS // 2):
            lo = slice(2 * p * HEAD_DIM, (2 * p + 1) * HEAD_DIM)
            hi = slice((2 * p + 1) * HEAD_DIM, (2 * p + 2) * HEAD_DIM)
            q2 = jnp.concatenate([q_ref[:, lo], q_ref[:, hi]], axis=0)
            g2 = jnp.concatenate([g_ref[:, lo], g_ref[:, hi]], axis=0)
            s = dot(q2, k, NT) * scale_log2
            own = jnp.where(seen, s[:, :BLOCK], -jnp.inf)
            s = jnp.concatenate([own, s[:, BLOCK:]], axis=1) if win > BLOCK else own
            top = jnp.max(s, axis=1, keepdims=True)
            e = jnp.exp2(s - top)
            share = e * (1.0 / jnp.sum(e, axis=1, keepdims=True))
            prob = share.astype(jnp.bfloat16)
            o = dot(prob, v, NN).astype(jnp.bfloat16)
            o_ref[:, lo] = o[:tok]
            o_ref[:, hi] = o[tok:]
            delta = jnp.sum(g2.astype(jnp.float32) * o.astype(jnp.float32), axis=1, keepdims=True)
            dp = dot(g2, v, NT)
            ds = (share * ((dp - delta) * scale)).astype(jnp.bfloat16)
            dq = dot(ds, k, NN).astype(jnp.bfloat16)
            dq_ref[:, lo] = dq[:tok]
            dq_ref[:, hi] = dq[tok:]
            part_k = dot(q2, ds, TN)
            part_v = dot(g2, prob, TN)
            if p == 0:
                acc_k[:, :win] = part_k
                acc_v[:, :win] = part_v
            else:
                acc_k[:, :win] += part_k
                acc_v[:, :win] += part_v

    for tiles in range(1, REACH + 2):
        pl.when(count == tiles)(functools.partial(work, tiles * BLOCK))

    for slot, acc in ((0, acc_k), (1, acc_v)):
        near[slot] = acc[:, :BLOCK].T
        for ref, back, place in zip((far_c, far_be, far_a, far_d), backs, places):

            @pl.when(back > 0)
            def _(slot=slot, acc=acc, ref=ref, place=place):
                ref[slot] = acc[:, place].T.astype(ref.dtype)

            @pl.when(back <= 0)
            def _(slot=slot, ref=ref):
                ref[slot] = jnp.zeros(ref.shape[1:], ref.dtype)


def attend(queries, grads, pieces, flags, inner):
    tok = queries.shape[0]
    key_width = pieces[0].shape[2]
    wide = pl.BlockSpec((tok, GROUPS * HEAD_DIM), lambda i: (0, i))
    piece = pl.BlockSpec((2, tok, HEAD_DIM), lambda i: (0, 0, i))
    smem = pl.BlockSpec(memory_space=pltpu.SMEM)
    win = (REACH + 1) * tok
    types = [jnp.bfloat16, jnp.bfloat16, jnp.float32, jnp.bfloat16, jnp.float32]
    return pl.pallas_call(
        attend_kernel,
        grid=(key_width // HEAD_DIM,),
        in_specs=[smem, smem, wide, wide] + [piece] * 6,
        out_specs=[wide, wide] + [piece] * 5,
        out_shape=[jax.ShapeDtypeStruct(queries.shape, jnp.bfloat16)] * 2
        + [jax.ShapeDtypeStruct((2, tok, key_width), t) for t in types],
        scratch_shapes=[
            pltpu.VMEM((win, HEAD_DIM), jnp.bfloat16),
            pltpu.VMEM((win, HEAD_DIM), jnp.bfloat16),
            pltpu.VMEM((HEAD_DIM, win), jnp.float32),
            pltpu.VMEM((HEAD_DIM, win), jnp.float32),
        ],
        compiler_params=pltpu.CompilerParams(vmem_limit_bytes=16 << 20),
        cost_estimate=pl.CostEstimate(
            flops=12 * queries.size * win,
            transcendentals=queries.size // HEAD_DIM * win,
            bytes_accessed=8 * queries.size + 18 * win * key_width * 2,
        ),
        name="attend",
    )(inner, flags, queries, grads, *pieces)


def deal_kernel(owner, tile_ref, _, own_ref, *outs):
    rows = own_ref.shape[0]
    for r, ref in enumerate((own_ref,) + outs):
        at = pl.ds(pl.multiple_of(owner[r] * rows, rows), rows)
        ref[...] = tile_ref[at, :].astype(ref.dtype)


def deal(owner, tile, token):
    vmem = pl.BlockSpec(memory_space=pltpu.VMEM)
    shape = (tile.shape[0] // 4, tile.shape[1])
    return pl.pallas_call(
        deal_kernel,
        in_specs=[pl.BlockSpec(memory_space=pltpu.SMEM), vmem, vmem],
        out_specs=[vmem] * 4,
        out_shape=[jax.ShapeDtypeStruct(shape, jnp.float32)]
        + [jax.ShapeDtypeStruct(shape, jnp.bfloat16)] * 3,
        compiler_params=pltpu.CompilerParams(vmem_limit_bytes=8 << 20),
        name="deal",
    )(owner, tile, token)


def outer_step(x, by):
    peers = lax.axis_size("ctx")
    by = by * INNER
    return lax.ppermute(x, "ctx", [(i, i + by) for i in range(peers) if 0 <= i + by < peers])


def to_inner(x, place):
    peers = lax.axis_size("ctx")
    return lax.ppermute(x, "ctx", [(i ^ 1, i) for i in range(peers) if i % INNER == place])


def outer_shift(x, by):
    peers = lax.axis_size("ctx")
    return lax.ppermute(x, "ctx", [(i, (i + INNER * by) % peers) for i in range(peers)])


def swap_inner(x):
    return lax.ppermute(x, "ctx", [(i, i ^ 1) for i in range(lax.axis_size("ctx"))])


def swap_fsdp(x):
    return lax.ppermute(x, "fsdp", [(0, 1), (1, 0)])


def swap_core(x):
    return lax.ppermute(x, "dp", [(0, 1), (1, 0)])


def odd_step(x, by):
    peers = lax.axis_size("ctx")
    start = 1 if by > 0 else 0
    return lax.ppermute(
        x, "ctx", [(i, i + by) for i in range(start, peers, 2) if 0 <= i + by < peers]
    )


def crossed(x, r, outer_core, plane_core=None):
    ctx, fsdp = lax.axis_size("ctx"), lax.axis_size("fsdp")
    flip_x, flip_y = PLANE[r]
    pairs = []
    for i in range(ctx):
        for j in range(fsdp):
            here = (i * fsdp + j) * 2
            if outer_core is not None:
                there = ((i + INNER * r) % ctx * fsdp + j) * 2
                pairs.append((here + outer_core, there + outer_core))
            if plane_core is not None:
                there = ((i ^ flip_x) * fsdp + (j ^ flip_y)) * 2
                pairs.append((here + plane_core, there + plane_core))
    return lax.ppermute(x, ("ctx", "fsdp", "dp"), pairs)


def split_kernel(offsets, mine_ref, theirs_ref, *refs):
    outs, held, in_sems, out_sems = refs[:4], refs[4], refs[5], refs[6]
    tok = mine_ref.shape[0]
    unit = held.shape[2] // 4
    reads = []
    for r in range(4):
        for k in range(4):
            at = pl.ds(pl.multiple_of(offsets[r, k] * unit, unit), unit)
            for i, src in enumerate((mine_ref, theirs_ref)):
                dst = held.at[r, pl.ds(i * tok, tok), pl.ds(k * unit, unit)]
                copy = pltpu.make_async_copy(src.at[:, at], dst, in_sems.at[r, k, i])
                copy.start()
                reads.append(copy)
    writes = []
    for r in range(4):
        for copy in reads[8 * r : 8 * r + 8]:
            copy.wait()
        writes.append(pltpu.make_async_copy(held.at[r], outs[r], out_sems.at[r]))
        writes[-1].start()
    for copy in writes:
        copy.wait()


def split(offsets, mine, theirs):
    hbm = pl.BlockSpec(memory_space=pltpu.HBM)
    tok, width = mine.shape
    shape = (2 * tok, width // 4)
    return pl.pallas_call(
        split_kernel,
        in_specs=[pl.BlockSpec(memory_space=pltpu.SMEM), hbm, hbm],
        out_specs=[hbm] * 4,
        out_shape=[jax.ShapeDtypeStruct(shape, mine.dtype)] * 4,
        scratch_shapes=[
            pltpu.VMEM((4,) + shape, mine.dtype),
            pltpu.SemaphoreType.DMA((4, 4, 2)),
            pltpu.SemaphoreType.DMA((4,)),
        ],
        compiler_params=pltpu.CompilerParams(vmem_limit_bytes=8 << 20),
        name="split",
    )(offsets, mine, theirs)


def per_device(inputs, queries, w_kv, tile_mask, grad_out):
    rows_in = inputs[0]
    tok, width = rows_in.shape
    rows, pair_width = w_kv.shape
    half = pair_width // 2
    ctx, fsdp, core = (lax.axis_index(a) for a in ("ctx", "fsdp", "dp"))
    outer = lax.axis_size("ctx") // INNER
    z, x = ctx // INNER, ctx % INNER
    order = list(range(outer))
    late, early = order[-1:], order[:-1]

    plane = [(x ^ i) * 2 + (fsdp ^ j) for i, j in ((0, 0), (1, 0), (0, 1), (1, 1))]
    spots = {r: [(z - r) % outer] + plane for r in order}

    def places(which):
        return jnp.stack([v for r in which for v in spots[r]]).astype(jnp.int32).reshape(-1, 5)

    mixed = outer == 4
    to_outer = [(z + r) % outer for r in range(outer)]
    to_plane = [(x ^ i) * 2 + (fsdp ^ j) for i, j in PLANE]
    cut = [jnp.where(core == 0, to_outer[r] * 4 + k, k * 4 + to_plane[r]) for r in range(4) for k in range(4)] if mixed else [x]
    known = {
        "cut": jnp.stack(cut).astype(jnp.int32).reshape(-1, 4 if mixed else 1),
        "owner": jnp.stack([jnp.where(core == 0, p, o) for p, o in zip(to_plane, to_outer)]).astype(jnp.int32),
        "early": places(early or late),
        "late": places(late),
        "flat": jnp.stack([spots[r][0] * 4 + v for r in order for v in plane]).astype(jnp.int32),
        "inner": x.reshape(1).astype(jnp.int32),
        "to": [((z + r) % outer) * (width // outer) for r in range(outer)],
        "half": core * half,
        "first": core == 0,
        "x": x,
        "not_x": 1 - x,
        "even": x == 0,
        "y": fsdp,
        "not_y": 1 - fsdp,
    }
    for k in ("half", "x", "not_x", "y", "not_y"):
        known[k] = known[k].astype(jnp.uint32)
    known["to"] = [t.astype(jnp.uint32) for t in known["to"]]
    known, w_kv = lax.optimization_barrier((known, w_kv))
    x, not_x, even, y, not_y, first_core = (
        known[k] for k in ("x", "not_x", "even", "y", "not_y", "first")
    )

    own = lax.dynamic_slice_in_dim(w_kv, known["half"], half, 1)
    theirs_in = swap_core(rows_in)
    tie = lax.optimization_barrier
    col, blocks, cols = own, {}, [own]
    for r in order:
        col_x = col_y = col
        if r == outer - 1 and r:
            col_x, blocks[r - 1][1] = tie((col, blocks[r - 1][1]))
            col_y, blocks[r - 1][2] = tie((col, blocks[r - 1][2]))
        following = outer_shift(col, 1) if r < outer - 1 else None
        by_x, by_y = swap_inner(col_x), swap_fsdp(col_y)
        if r == 0 and mixed:
            early_cuts = split(known["cut"], rows_in, theirs_in)
            following, by_x, by_y, early_cuts = tie((following, by_x, by_y, early_cuts))
        elif r == 1 and outer > 2:
            following, by_x = tie((following, by_x))
        blocks[r] = [col, by_x, by_y]
        col = following
        cols.append(col)
    for r in order:
        if r == 0:
            diagonal = swap_fsdp(blocks[0][1])
        elif r == outer - 1:
            diagonal = swap_inner(blocks[r][2])
        else:
            diagonal = outer_shift(diagonal, 1)
        blocks[r].append(diagonal)

    def listed(which):
        return [v for r in which for v in blocks[r]]

    by_blocks = rows % 128 == 0
    if by_blocks:
        part_sum = project(known["early"], rows_in, theirs_in, listed(early), None, jnp.float32)
        kv = project(known["late"], rows_in, theirs_in, listed(late), part_sum, jnp.bfloat16)
    else:
        weight_half = jnp.zeros((width, half), w_kv.dtype)
        for i, block in enumerate(listed(order)):
            at = known["flat"][i] * rows
            weight_half = lax.dynamic_update_slice_in_dim(weight_half, block, at, 0)
        kv = dot(jnp.concatenate([rows_in, theirs_in], axis=0), weight_half, NN).astype(jnp.bfloat16)
    block = width // outer

    def columns(t, r):
        return lax.dynamic_slice_in_dim(t, known["to"][r], block, 1)

    if mixed:
        cuts = early_cuts
    else:
        in_mine = [outer_shift(columns(rows_in, r), r) for r in range(1, outer)]
        in_theirs = [columns(theirs_in, 0)] + [swap_core(t) for t in in_mine]
        in_mine = [columns(rows_in, 0)] + in_mine

    mine, theirs = kv[:tok], swap_core(kv[tok:])
    key_vals = jnp.where(first_core, jnp.stack([mine, theirs]), jnp.stack([theirs, mine]))

    back_a = outer_step(key_vals, 1)
    back_b = to_inner(key_vals, 1)
    if by_blocks:
        tied = tie((*listed(order), kv))
        weight_half = assemble(known["flat"], list(tied[:-1]))
        weight_half, back_a = tie((weight_half, back_a))
    back_c = outer_step(back_a, 1)
    back_d = swap_inner(back_a)
    back_e = odd_step(back_a, 1)
    weight_other = swap_core(weight_half)

    if mixed:
        late_cuts, back_d = tie((cuts[1:], back_d))
        passed = [crossed(late_cuts[r - 1], r, 0, 1) for r in range(1, 4)]
    attended, grad_query, far_c, far_be, far_a, far_d, near = attend(
        queries[0],
        grad_out[0],
        [back_c, back_b, back_e, back_a, back_d, key_vals],
        tile_mask,
        known["inner"],
    )
    got_c = outer_step(far_c, -1).astype(jnp.float32)
    got_e = odd_step(far_be, -1).astype(jnp.float32)
    got_d = swap_inner(far_d).astype(jnp.float32)
    got_b = to_inner(far_be, 0).astype(jnp.float32)
    if mixed:
        far_a, passed = tie((far_a, passed))
    sent_a = (far_a + got_d + got_c + got_e).astype(jnp.bfloat16)
    got_a = outer_step(sent_a, -1).astype(jnp.float32)
    grad_kv = (near + got_b + got_a).astype(jnp.bfloat16)
    grad_mine = jnp.where(first_core, grad_kv[0], grad_kv[1])
    grad_theirs = jnp.where(first_core, grad_kv[1], grad_kv[0])

    grad_in = (dot(grad_mine, weight_half, NT) + dot(grad_theirs, weight_other, NT)).astype(
        jnp.bfloat16
    )

    grad_pair = jnp.concatenate([grad_mine, swap_core(grad_theirs)], axis=0)
    if mixed:
        in_both = [cuts[0]] + passed
    else:
        in_both = [jnp.concatenate(t, axis=0) for t in zip(in_mine, in_theirs)]
    tile = None
    for r in range(outer):
        gathered = grad_pair
        if r:
            gathered = crossed(grad_pair, r, 0, 1) if mixed else outer_shift(grad_pair, r)
        term = dot(in_both[r], gathered, TN)
        tile = term if tile is None else tile + term

    def pick(t, index, axis):
        return lax.dynamic_index_in_dim(t, index, axis, keepdims=False)

    def sent(t, swap):
        return swap(t.astype(jnp.bfloat16)).astype(jnp.float32)

    if mixed:
        token = swap_core(tile[:8, :HEAD_DIM])
        grad_half, *leaving = deal(known["owner"], tile, token)
        arrived = [crossed(leaving[r - 1], r, 1, 0) for r in range(1, 4)]
        arrived, grad_in = tie((arrived, grad_in))
        for t in arrived:
            grad_half += t.astype(jnp.float32)
    else:
        tile = tile.reshape(2, 2, rows, half)
        first, second = tile[..., : half // 2], tile[..., half // 2 :]
        first = pick(first, x, 0) + sent(pick(first, not_x, 0), swap_inner)
        second = pick(second, y, 1) + sent(pick(second, not_y, 1), swap_fsdp)
        first = pick(first, y, 0) + sent(pick(first, not_y, 0), swap_fsdp)
        second = pick(second, x, 0) + sent(pick(second, not_x, 0), swap_inner)
        grad_half = jnp.concatenate([first, second], axis=1)
    tokens = lax.axis_size("fsdp") * lax.axis_size("dp") * lax.axis_size("ctx") * tok
    grad_half = grad_half * (1.0 / math.sqrt(tokens))
    grad_rest = swap_core(grad_half)
    weight_grad = jnp.where(
        first_core,
        jnp.concatenate([grad_half, grad_rest], axis=1),
        jnp.concatenate([grad_rest, grad_half], axis=1),
    )
    return (attended[None], grad_query[None], grad_in[None], weight_grad)


def solution(mesh):
    return jax.shard_map(
        per_device,
        mesh=mesh,
        in_specs=(
            P(("fsdp", "dp"), "ctx", None),
            P(("fsdp", "dp"), "ctx", None),
            P(("ctx", "fsdp"), None),
            P("ctx", None),
            P(("fsdp", "dp"), "ctx", None),
        ),
        out_specs=(
            P(("fsdp", "dp"), "ctx", None),
            P(("fsdp", "dp"), "ctx", None),
            P(("fsdp", "dp"), "ctx", None),
            P(("ctx", "fsdp"), None),
        ),
        check_vma=False,
    )
```

```python
import functools
import math

import jax
import jax.numpy as jnp
from jax import lax
from jax.experimental import pallas as pl
from jax.experimental.pallas import tpu as pltpu
from jax.sharding import PartitionSpec as P

HEADS = 32
KV_HEADS = 4
HEAD_DIM = 128
BLOCK = 128
REACH = 4
GROUPS = HEADS // KV_HEADS
INNER = 2
PLANE = ((0, 0), (1, 1), (1, 0), (0, 1))

NT = (((1,), (1,)), ((), ()))
NN = (((1,), (0,)), ((), ()))
TN = (((0,), (0,)), ((), ()))


def dot(a, b, dims):
    return lax.dot_general(a, b, dims, preferred_element_type=jnp.float32)


def project_kernel(count, spots, mine_ref, theirs_ref, *refs):
    blocks = refs[:count]
    carry = refs[count] if len(refs) > count + 6 else None
    out_ref, lhs, total, rhs, lhs_sems, rhs_sems = refs[-6:]
    tok = mine_ref.shape[0]
    groups, _, group = lhs.shape
    unit = rhs.shape[2]
    copies, fetches = [], []
    for g in range(groups):
        at = pl.ds(pl.multiple_of(spots[g, 0] * group, group), group)
        for i, src in enumerate((mine_ref, theirs_ref)):
            rows = pl.ds(i * tok, tok)
            copies.append(
                pltpu.make_async_copy(src.at[:, at], lhs.at[g, rows, :], lhs_sems.at[g, i])
            )
            copies[-1].start()
        for kind in range(4):
            j = 4 * g + kind
            fetches.append(pltpu.make_async_copy(blocks[j], rhs.at[g, kind], rhs_sems.at[j]))
            fetches[-1].start()
    if carry is None:
        total[...] = jnp.zeros_like(total)
    else:
        total[...] = carry[...]
    for g in range(groups):
        copies[2 * g].wait()
        copies[2 * g + 1].wait()
        for kind in range(4):
            fetches[4 * g + kind].wait()
            at = pl.ds(pl.multiple_of(spots[g, 1 + kind] * unit, unit), unit)
            total[...] += dot(lhs[g, :, at], rhs[g, kind], NN)
    out_ref[...] = total[...].astype(out_ref.dtype)


def project(spots, mine, theirs, blocks, carry, out_type):
    vmem = pl.BlockSpec(memory_space=pltpu.VMEM)
    hbm = pl.BlockSpec(memory_space=pltpu.HBM)
    extra = [] if carry is None else [carry]
    tok = mine.shape[0]
    rows, half = blocks[0].shape
    groups = len(blocks) // 4
    return pl.pallas_call(
        functools.partial(project_kernel, len(blocks)),
        in_specs=[pl.BlockSpec(memory_space=pltpu.SMEM)]
        + [hbm] * (2 + len(blocks))
        + [vmem] * len(extra),
        out_specs=vmem,
        out_shape=jax.ShapeDtypeStruct((2 * tok, half), out_type),
        scratch_shapes=[
            pltpu.VMEM((groups, 2 * tok, 4 * rows), mine.dtype),
            pltpu.VMEM((2 * tok, half), jnp.float32),
            pltpu.VMEM((groups, 4, rows, half), mine.dtype),
            pltpu.SemaphoreType.DMA((groups, 2)),
            pltpu.SemaphoreType.DMA((len(blocks),)),
        ],
        compiler_params=pltpu.CompilerParams(vmem_limit_bytes=16 << 20),
        name="project",
    )(spots, mine, theirs, *blocks, *extra)


def assemble_kernel(spots, *refs):
    blocks = refs[:-4]
    out_ref, held, sems, out_sem = refs[-4:]
    unit = blocks[0].shape[0]
    copies = []
    for j, block in enumerate(blocks):
        at = pl.ds(pl.multiple_of(spots[j] * unit, unit), unit)
        copies.append(pltpu.make_async_copy(block, held.at[at, :], sems.at[j]))
        copies[-1].start()
    for copy in copies:
        copy.wait()
    write = pltpu.make_async_copy(held, out_ref, out_sem)
    write.start()
    write.wait()


def assemble(spots, blocks):
    hbm = pl.BlockSpec(memory_space=pltpu.HBM)
    rows = sum(b.shape[0] for b in blocks)
    shape = (rows, blocks[0].shape[1])
    return pl.pallas_call(
        assemble_kernel,
        in_specs=[pl.BlockSpec(memory_space=pltpu.SMEM)] + [hbm] * len(blocks),
        out_specs=hbm,
        out_shape=jax.ShapeDtypeStruct(shape, blocks[0].dtype),
        scratch_shapes=[
            pltpu.VMEM(shape, blocks[0].dtype),
            pltpu.SemaphoreType.DMA((len(blocks),)),
            pltpu.SemaphoreType.DMA,
        ],
        compiler_params=pltpu.CompilerParams(vmem_limit_bytes=16 << 20),
        name="assemble",
    )(spots, *blocks)


def attend_kernel(inner, flags, q_ref, g_ref, *refs):
    c_ref, b_ref, e_ref, a_ref, d_ref, own_ref = refs[:6]
    o_ref, dq_ref, far_c, far_be, far_a, far_d, near = refs[6:13]
    k_held, v_held, acc_k, acc_v, sum_k, sum_v = refs[13:]
    tok = q_ref.shape[0]
    scale = 1.0 / math.sqrt(HEAD_DIM)
    scale_log2 = scale * math.log2(math.e)
    even = inner[0] == 0
    backs = (
        flags[0, 3],
        jnp.where(even, flags[0, 2], flags[0, 0]),
        flags[0, 1],
        jnp.where(even, flags[0, 0], flags[0, 2]),
    )
    count, places = jnp.int32(1), []
    for back in backs:
        places.append(pl.ds(pl.multiple_of(count * BLOCK, BLOCK), BLOCK))
        count = count + jnp.where(back > 0, 1, 0)

    k_held[:BLOCK], v_held[:BLOCK] = own_ref[0], own_ref[1]
    for j, (back, place) in enumerate(zip(backs, places)):

        @pl.when(back > 0)
        def _(j=j, place=place):
            for slot, held in ((0, k_held), (1, v_held)):
                if j == 1:
                    held[place, :] = jnp.where(even, e_ref[slot], b_ref[slot])
                else:
                    held[place, :] = (c_ref, None, a_ref, d_ref)[j][slot]

    def work(win):
        k, v = k_held[:win], v_held[:win]
        row = lax.broadcasted_iota(jnp.int32, (2 * tok, BLOCK), 0) % tok
        col = lax.broadcasted_iota(jnp.int32, (2 * tok, BLOCK), 1)
        seen = col <= row
        for p in range(GROUPS // 2):
            lo = slice(2 * p * HEAD_DIM, (2 * p + 1) * HEAD_DIM)
            hi = slice((2 * p + 1) * HEAD_DIM, (2 * p + 2) * HEAD_DIM)
            q2 = jnp.concatenate([q_ref[:, lo], q_ref[:, hi]], axis=0)
            g2 = jnp.concatenate([g_ref[:, lo], g_ref[:, hi]], axis=0)
            s = dot(q2, k, NT) * scale_log2
            own = jnp.where(seen, s[:, :BLOCK], -jnp.inf)
            s = jnp.concatenate([own, s[:, BLOCK:]], axis=1) if win > BLOCK else own
            top = jnp.max(s, axis=1, keepdims=True)
            e = jnp.exp2(s - top)
            share = e * (1.0 / jnp.sum(e, axis=1, keepdims=True))
            prob = share.astype(jnp.bfloat16)
            o = dot(prob, v, NN).astype(jnp.bfloat16)
            o_ref[:, lo] = o[:tok]
            o_ref[:, hi] = o[tok:]
            delta = jnp.sum(g2.astype(jnp.float32) * o.astype(jnp.float32), axis=1, keepdims=True)
            dp = dot(g2, v, NT)
            ds = (share * ((dp - delta) * scale)).astype(jnp.bfloat16)
            dq = dot(ds, k, NN).astype(jnp.bfloat16)
            dq_ref[:, lo] = dq[:tok]
            dq_ref[:, hi] = dq[tok:]
            part_k = dot(q2, ds, TN)
            part_v = dot(g2, prob, TN)
            if p == 0:
                acc_k[:, :win] = part_k
                acc_v[:, :win] = part_v
            elif p < GROUPS // 2 - 1:
                acc_k[:, :win] += part_k
                acc_v[:, :win] += part_v
            else:
                sum_k[:win] = (acc_k[:, :win] + part_k).T
                sum_v[:win] = (acc_v[:, :win] + part_v).T

    for tiles in range(1, REACH + 2):
        pl.when(count == tiles)(functools.partial(work, tiles * BLOCK))

    near[0], near[1] = sum_k[:BLOCK], sum_v[:BLOCK]
    for ref, back, place in zip((far_c, far_be, far_a, far_d), backs, places):

        @pl.when(back > 0)
        def _(ref=ref, place=place):
            ref[0] = sum_k[place, :].astype(ref.dtype)
            ref[1] = sum_v[place, :].astype(ref.dtype)

        @pl.when(back <= 0)
        def _(ref=ref):
            ref[...] = jnp.zeros(ref.shape, ref.dtype)


def attend(queries, grads, pieces, flags, inner):
    tok = queries.shape[0]
    key_width = pieces[0].shape[2]
    wide = pl.BlockSpec((tok, GROUPS * HEAD_DIM), lambda i: (0, i))
    piece = pl.BlockSpec((2, tok, HEAD_DIM), lambda i: (0, 0, i))
    smem = pl.BlockSpec(memory_space=pltpu.SMEM)
    win = (REACH + 1) * tok
    types = [jnp.bfloat16, jnp.bfloat16, jnp.float32, jnp.bfloat16, jnp.float32]
    return pl.pallas_call(
        attend_kernel,
        grid=(key_width // HEAD_DIM,),
        in_specs=[smem, smem, wide, wide] + [piece] * 6,
        out_specs=[wide, wide] + [piece] * 5,
        out_shape=[jax.ShapeDtypeStruct(queries.shape, jnp.bfloat16)] * 2
        + [jax.ShapeDtypeStruct((2, tok, key_width), t) for t in types],
        scratch_shapes=[
            pltpu.VMEM((win, HEAD_DIM), jnp.bfloat16),
            pltpu.VMEM((win, HEAD_DIM), jnp.bfloat16),
            pltpu.VMEM((HEAD_DIM, win), jnp.float32),
            pltpu.VMEM((HEAD_DIM, win), jnp.float32),
            pltpu.VMEM((win, HEAD_DIM), jnp.float32),
            pltpu.VMEM((win, HEAD_DIM), jnp.float32),
        ],
        compiler_params=pltpu.CompilerParams(vmem_limit_bytes=16 << 20),
        cost_estimate=pl.CostEstimate(
            flops=12 * queries.size * win,
            transcendentals=queries.size // HEAD_DIM * win,
            bytes_accessed=8 * queries.size + 18 * win * key_width * 2,
        ),
        name="attend",
    )(inner, flags, queries, grads, *pieces)


def deal_kernel(owner, tile_ref, _, own_ref, *outs):
    rows = own_ref.shape[0]
    for r, ref in enumerate((own_ref,) + outs):
        at = pl.ds(pl.multiple_of(owner[r] * rows, rows), rows)
        ref[...] = tile_ref[at, :].astype(ref.dtype)


def deal(owner, tile, token):
    vmem = pl.BlockSpec(memory_space=pltpu.VMEM)
    shape = (tile.shape[0] // 4, tile.shape[1])
    return pl.pallas_call(
        deal_kernel,
        in_specs=[pl.BlockSpec(memory_space=pltpu.SMEM), vmem, vmem],
        out_specs=[vmem] * 4,
        out_shape=[jax.ShapeDtypeStruct(shape, jnp.float32)]
        + [jax.ShapeDtypeStruct(shape, jnp.bfloat16)] * 3,
        compiler_params=pltpu.CompilerParams(vmem_limit_bytes=8 << 20),
        name="deal",
    )(owner, tile, token)


def outer_step(x, by):
    peers = lax.axis_size("ctx")
    by = by * INNER
    return lax.ppermute(x, "ctx", [(i, i + by) for i in range(peers) if 0 <= i + by < peers])


def to_inner(x, place):
    peers = lax.axis_size("ctx")
    return lax.ppermute(x, "ctx", [(i ^ 1, i) for i in range(peers) if i % INNER == place])


def outer_shift(x, by):
    peers = lax.axis_size("ctx")
    return lax.ppermute(x, "ctx", [(i, (i + INNER * by) % peers) for i in range(peers)])


def swap_inner(x):
    return lax.ppermute(x, "ctx", [(i, i ^ 1) for i in range(lax.axis_size("ctx"))])


def swap_fsdp(x):
    return lax.ppermute(x, "fsdp", [(0, 1), (1, 0)])


def swap_core(x):
    return lax.ppermute(x, "dp", [(0, 1), (1, 0)])


def odd_step(x, by):
    peers = lax.axis_size("ctx")
    start = 1 if by > 0 else 0
    return lax.ppermute(
        x, "ctx", [(i, i + by) for i in range(start, peers, 2) if 0 <= i + by < peers]
    )


def crossed(x, r, outer_core, plane_core=None):
    ctx, fsdp = lax.axis_size("ctx"), lax.axis_size("fsdp")
    flip_x, flip_y = PLANE[r]
    pairs = []
    for i in range(ctx):
        for j in range(fsdp):
            here = (i * fsdp + j) * 2
            if outer_core is not None:
                there = ((i + INNER * r) % ctx * fsdp + j) * 2
                pairs.append((here + outer_core, there + outer_core))
            if plane_core is not None:
                there = ((i ^ flip_x) * fsdp + (j ^ flip_y)) * 2
                pairs.append((here + plane_core, there + plane_core))
    return lax.ppermute(x, ("ctx", "fsdp", "dp"), pairs)


def split_kernel(offsets, mine_ref, theirs_ref, *refs):
    outs, held, in_sems, out_sems = refs[:4], refs[4], refs[5], refs[6]
    tok = mine_ref.shape[0]
    unit = held.shape[2] // 4
    reads = []
    for r in range(4):
        for k in range(4):
            at = pl.ds(pl.multiple_of(offsets[r, k] * unit, unit), unit)
            for i, src in enumerate((mine_ref, theirs_ref)):
                dst = held.at[r, pl.ds(i * tok, tok), pl.ds(k * unit, unit)]
                copy = pltpu.make_async_copy(src.at[:, at], dst, in_sems.at[r, k, i])
                copy.start()
                reads.append(copy)
    writes = []
    for r in range(4):
        for copy in reads[8 * r : 8 * r + 8]:
            copy.wait()
        writes.append(pltpu.make_async_copy(held.at[r], outs[r], out_sems.at[r]))
        writes[-1].start()
    for copy in writes:
        copy.wait()


def split(offsets, mine, theirs):
    hbm = pl.BlockSpec(memory_space=pltpu.HBM)
    tok, width = mine.shape
    shape = (2 * tok, width // 4)
    return pl.pallas_call(
        split_kernel,
        in_specs=[pl.BlockSpec(memory_space=pltpu.SMEM), hbm, hbm],
        out_specs=[hbm] * 4,
        out_shape=[jax.ShapeDtypeStruct(shape, mine.dtype)] * 4,
        scratch_shapes=[
            pltpu.VMEM((4,) + shape, mine.dtype),
            pltpu.SemaphoreType.DMA((4, 4, 2)),
            pltpu.SemaphoreType.DMA((4,)),
        ],
        compiler_params=pltpu.CompilerParams(vmem_limit_bytes=8 << 20),
        name="split",
    )(offsets, mine, theirs)


def per_device(inputs, queries, w_kv, tile_mask, grad_out):
    rows_in = inputs[0]
    tok, width = rows_in.shape
    rows, pair_width = w_kv.shape
    half = pair_width // 2
    ctx, fsdp, core = (lax.axis_index(a) for a in ("ctx", "fsdp", "dp"))
    outer = lax.axis_size("ctx") // INNER
    z, x = ctx // INNER, ctx % INNER
    order = list(range(outer))
    late, early = order[-1:], order[:-1]

    plane = [(x ^ i) * 2 + (fsdp ^ j) for i, j in ((0, 0), (1, 0), (0, 1), (1, 1))]
    spots = {r: [(z - r) % outer] + plane for r in order}

    def places(which):
        return jnp.stack([v for r in which for v in spots[r]]).astype(jnp.int32).reshape(-1, 5)

    mixed = outer == 4
    to_outer = [(z + r) % outer for r in range(outer)]
    to_plane = [(x ^ i) * 2 + (fsdp ^ j) for i, j in PLANE]
    cut = [jnp.where(core == 0, to_outer[r] * 4 + k, k * 4 + to_plane[r]) for r in range(4) for k in range(4)] if mixed else [x]
    known = {
        "cut": jnp.stack(cut).astype(jnp.int32).reshape(-1, 4 if mixed else 1),
        "owner": jnp.stack([jnp.where(core == 0, p, o) for p, o in zip(to_plane, to_outer)]).astype(jnp.int32),
        "early": places(early or late),
        "late": places(late),
        "flat": jnp.stack([spots[r][0] * 4 + v for r in order for v in plane]).astype(jnp.int32),
        "inner": x.reshape(1).astype(jnp.int32),
        "to": [((z + r) % outer) * (width // outer) for r in range(outer)],
        "half": core * half,
        "first": core == 0,
        "x": x,
        "not_x": 1 - x,
        "even": x == 0,
        "y": fsdp,
        "not_y": 1 - fsdp,
    }
    for k in ("half", "x", "not_x", "y", "not_y"):
        known[k] = known[k].astype(jnp.uint32)
    known["to"] = [t.astype(jnp.uint32) for t in known["to"]]
    known, w_kv = lax.optimization_barrier((known, w_kv))
    x, not_x, even, y, not_y, first_core = (
        known[k] for k in ("x", "not_x", "even", "y", "not_y", "first")
    )

    own = lax.dynamic_slice_in_dim(w_kv, known["half"], half, 1)
    theirs_in = swap_core(rows_in)
    tie = lax.optimization_barrier
    col, blocks, cols = own, {}, [own]
    for r in order:
        col_x = col_y = col
        if r == outer - 1 and r:
            col_x, blocks[r - 1][1] = tie((col, blocks[r - 1][1]))
            col_y, blocks[r - 1][2] = tie((col, blocks[r - 1][2]))
        following = outer_shift(col, 1) if r < outer - 1 else None
        by_x, by_y = swap_inner(col_x), swap_fsdp(col_y)
        if r == 0 and mixed:
            early_cuts = split(known["cut"], rows_in, theirs_in)
            following, by_x, by_y, early_cuts = tie((following, by_x, by_y, early_cuts))
        elif r == 1 and outer > 2:
            following, by_x = tie((following, by_x))
        blocks[r] = [col, by_x, by_y]
        col = following
        cols.append(col)
    for r in order:
        if r == 0:
            diagonal = swap_fsdp(blocks[0][1])
        elif r == outer - 1:
            diagonal = swap_inner(blocks[r][2])
        else:
            diagonal = outer_shift(diagonal, 1)
        blocks[r].append(diagonal)

    def listed(which):
        return [v for r in which for v in blocks[r]]

    by_blocks = rows % 128 == 0
    if by_blocks:
        part_sum = project(known["early"], rows_in, theirs_in, listed(early), None, jnp.float32)
        kv = project(known["late"], rows_in, theirs_in, listed(late), part_sum, jnp.bfloat16)
    else:
        weight_half = jnp.zeros((width, half), w_kv.dtype)
        for i, block in enumerate(listed(order)):
            at = known["flat"][i] * rows
            weight_half = lax.dynamic_update_slice_in_dim(weight_half, block, at, 0)
        kv = dot(jnp.concatenate([rows_in, theirs_in], axis=0), weight_half, NN).astype(jnp.bfloat16)
    block = width // outer

    def columns(t, r):
        return lax.dynamic_slice_in_dim(t, known["to"][r], block, 1)

    if mixed:
        cuts = early_cuts
    else:
        in_mine = [outer_shift(columns(rows_in, r), r) for r in range(1, outer)]
        in_theirs = [columns(theirs_in, 0)] + [swap_core(t) for t in in_mine]
        in_mine = [columns(rows_in, 0)] + in_mine

    mine, theirs = kv[:tok], swap_core(kv[tok:])
    key_vals = jnp.where(first_core, jnp.stack([mine, theirs]), jnp.stack([theirs, mine]))

    back_a = outer_step(key_vals, 1)
    back_b = to_inner(key_vals, 1)
    if by_blocks:
        tied = tie((*listed(order), kv))
        weight_half = assemble(known["flat"], list(tied[:-1]))
        weight_half, back_a = tie((weight_half, back_a))
    back_c = outer_step(back_a, 1)
    back_d = swap_inner(back_a)
    back_e = odd_step(back_a, 1)
    weight_other = swap_core(weight_half)

    if mixed:
        late_cuts, back_d = tie((cuts[1:], back_d))
        passed = [crossed(late_cuts[r - 1], r, 0, 1) for r in range(1, 4)]
    attended, grad_query, far_c, far_be, far_a, far_d, near = attend(
        queries[0],
        grad_out[0],
        [back_c, back_b, back_e, back_a, back_d, key_vals],
        tile_mask,
        known["inner"],
    )
    got_c = outer_step(far_c, -1).astype(jnp.float32)
    got_e = odd_step(far_be, -1).astype(jnp.float32)
    got_d = swap_inner(far_d).astype(jnp.float32)
    got_b = to_inner(far_be, 0).astype(jnp.float32)
    if mixed:
        far_a, passed = tie((far_a, passed))
    sent_a = (far_a + got_d + got_c + got_e).astype(jnp.bfloat16)
    got_a = outer_step(sent_a, -1).astype(jnp.float32)
    grad_kv = (near + got_b + got_a).astype(jnp.bfloat16)
    grad_mine = jnp.where(first_core, grad_kv[0], grad_kv[1])
    grad_theirs = jnp.where(first_core, grad_kv[1], grad_kv[0])

    grad_in = (dot(grad_mine, weight_half, NT) + dot(grad_theirs, weight_other, NT)).astype(
        jnp.bfloat16
    )

    grad_pair = jnp.concatenate([grad_mine, swap_core(grad_theirs)], axis=0)
    if mixed:
        in_both = [cuts[0]] + passed
    else:
        in_both = [jnp.concatenate(t, axis=0) for t in zip(in_mine, in_theirs)]
    tile = None
    for r in range(outer):
        gathered = grad_pair
        if r:
            gathered = crossed(grad_pair, r, 0, 1) if mixed else outer_shift(grad_pair, r)
        term = dot(in_both[r], gathered, TN)
        tile = term if tile is None else tile + term

    def pick(t, index, axis):
        return lax.dynamic_index_in_dim(t, index, axis, keepdims=False)

    def sent(t, swap):
        return swap(t.astype(jnp.bfloat16)).astype(jnp.float32)

    if mixed:
        token = swap_core(tile[:8, :HEAD_DIM])
        grad_half, *leaving = deal(known["owner"], tile, token)
        arrived = [crossed(leaving[r - 1], r, 1, 0) for r in range(1, 4)]
        arrived, grad_in = tie((arrived, grad_in))
        for t in arrived:
            grad_half += t.astype(jnp.float32)
    else:
        tile = tile.reshape(2, 2, rows, half)
        first, second = tile[..., : half // 2], tile[..., half // 2 :]
        first = pick(first, x, 0) + sent(pick(first, not_x, 0), swap_inner)
        second = pick(second, y, 1) + sent(pick(second, not_y, 1), swap_fsdp)
        first = pick(first, y, 0) + sent(pick(first, not_y, 0), swap_fsdp)
        second = pick(second, x, 0) + sent(pick(second, not_x, 0), swap_inner)
        grad_half = jnp.concatenate([first, second], axis=1)
    tokens = lax.axis_size("fsdp") * lax.axis_size("dp") * lax.axis_size("ctx") * tok
    grad_half = grad_half * (1.0 / math.sqrt(tokens))
    grad_rest = swap_core(grad_half)
    weight_grad = jnp.where(
        first_core,
        jnp.concatenate([grad_half, grad_rest], axis=1),
        jnp.concatenate([grad_rest, grad_half], axis=1),
    )
    return (attended[None], grad_query[None], grad_in[None], weight_grad)


def solution(mesh):
    return jax.shard_map(
        per_device,
        mesh=mesh,
        in_specs=(
            P(("fsdp", "dp"), "ctx", None),
            P(("fsdp", "dp"), "ctx", None),
            P(("ctx", "fsdp"), None),
            P("ctx", None),
            P(("fsdp", "dp"), "ctx", None),
        ),
        out_specs=(
            P(("fsdp", "dp"), "ctx", None),
            P(("fsdp", "dp"), "ctx", None),
            P(("fsdp", "dp"), "ctx", None),
            P(("ctx", "fsdp"), None),
        ),
        check_vma=False,
    )
```
